128 devices in a mesh: group: 4 (over z_hi, core), blk: 32 (over x, y, z_lo).
Axes of the slice: x: 4, y: 4, z: 4 (z_hi: 2, z_lo: 2; z = z_hi * 2 + z_lo), core: 2. Of those that a mesh axis runs over, the one named last changes fastest.
Arguments:
- vertex: float32 [131072, 256], P(('group', 'blk')), may hold values from -1.5 to 1.5
- vertex_state: float32 [131072], P(('group', 'blk')), may hold values from 0.1 to 1
- context: float32 [65536, 256], P(('group', 'blk')), may hold values from -1.5 to 1.5
- context_state: float32 [65536], P(('group', 'blk')), may hold values from 0.1 to 1
- tile_weights: bfloat16 [4, 32, 4, 6, 3, 128, 128], P('group', 'blk'), may hold values from 0.049804688 to 2
- tile_rows: int32 [4, 32, 4, 6, 3], P('group', 'blk'), may hold values from 0 to 7
- tile_cols: int32 [4, 32, 4, 6, 3], P('group', 'blk'), may hold values from 0 to 3
- tile_counts: int32 [4, 32, 4, 6], P('group', 'blk'), may hold values from 1 to 3, as said below
- negatives: int32 [4, 32, 6, 8, 2], P('group', 'blk'), may hold values from 0 to 3
Outputs:
- vertex_out: float32 [131072, 256], P(('group', 'blk'))
- vertex_state_out: float32 [131072], P(('group', 'blk'))
- context_out: float32 [65536, 256], P(('group', 'blk'))
- context_state_out: float32 [65536], P(('group', 'blk'))
The draws below stay inside these ranges and needn't reach their ends.
Inputs may be any that keep to these rules, and one draw needn't show every extreme that they name: `tile_counts`: at each stop and each index of blk some destination of the group receives 3 used slots from every walk owner.
All inputs are finite; a program needn't handle non-finite values.
Results may differ from the reference program's by a relative error of at most 0.0049.
Values may be sent and summed in bfloat16 or wider, within the bound.
No kernel may reach another device: no remote copies, remote signals or barrier semaphores. Data moves between devices by JAX's collectives and lax.ppermute only.
A program may use at most 64 MiB of HBM per device.

```python
import math
import jax
import jax.numpy as jnp
from jax import lax

D = 256
TILE = 128
CTX = 512
R_DEV = 1024
STEPS = 6
CAP = 3
NNEG = 2
RT = 8
CT = 4
NV = 131072
NC = 65536
N_GROUP = 4
N_BLK = 32


def draw_tile_counts(key, part):
    first = jax.random.fold_in(key, 71)
    second = jax.random.fold_in(key, 72)
    base = jax.random.randint(first, (N_GROUP, N_BLK, N_GROUP, STEPS), 1, CAP + 1)
    chosen = jax.random.randint(second, (1, N_BLK, 1, STEPS), 0, N_GROUP)
    target = jnp.arange(N_GROUP)[None, None, :, None]
    return jnp.where(target == chosen, CAP, base).astype(jnp.int32)


def touch_ends(array, stream_key, smallest, top_value):
    spot = [jax.random.randint(jax.random.fold_in(stream_key, axis), (), 0, length) for axis, length in enumerate(array.shape)]
    longest = array.shape.index(max(array.shape))
    next_to = spot[:longest] + [(spot[longest] + 1) % array.shape[longest]] + spot[longest + 1:]
    return array.at[tuple(spot)].set(smallest).at[tuple(next_to)].set(top_value)


def block_scale(rng, dims, pieces, low, largest):
    gain = 1.0
    for position, blocks in pieces:
        heights = jax.random.uniform(jax.random.fold_in(jax.random.fold_in(rng, 6), position), (blocks,), jnp.float32, low / len(pieces), largest / len(pieces))
        gain = gain * jnp.repeat(jnp.exp(heights), dims[position] // blocks).reshape((-1,) + (1,) * (len(dims) - 1 - position))
    return gain


def gaussian(rng, shape, spread, bound, pieces=(), kind=jnp.bfloat16):
    entries = spread * jax.random.normal(rng, shape, jnp.float32)
    if pieces:
        entries = entries * block_scale(rng, shape, pieces, -0.22, 0.18)
    return jnp.clip(entries, -bound, bound).astype(kind)


def setup_inputs(seed: int = 0) -> dict:
    key_of = jax.random.split(jax.random.key(seed), 10)
    return {
        "vertex": gaussian(key_of[0], (NV, D), 0.25, 1.5, ((0, 128),), jnp.float32),
        "vertex_state": jnp.clip(jnp.exp(math.log(1.0) - 2.3025851 * jax.random.uniform(key_of[1], (NV,), jnp.float32) ** block_scale(key_of[1], (NV,), ((0, 128),), -0.2, 0.2)), 0.1, 1.0),
        "context": gaussian(key_of[2], (NC, D), 0.25, 1.5, ((0, 128),), jnp.float32),
        "context_state": jnp.clip(jnp.exp(math.log(1.0) - 2.3025851 * jax.random.uniform(key_of[3], (NC,), jnp.float32) ** block_scale(key_of[3], (NC,), ((0, 128),), -0.2, 0.2)), 0.1, 1.0),
        "tile_weights": jnp.clip(jnp.exp(math.log(2.0) - 3.6927934 * jax.random.uniform(key_of[4], (N_GROUP, N_BLK, N_GROUP, STEPS, CAP, TILE, TILE), jnp.float32) ** block_scale(key_of[4], (N_GROUP, N_BLK, N_GROUP, STEPS, CAP, TILE, TILE), ((0, 4), (1, 32)), -0.2, 0.2)), 0.049804688, 2.0).astype(jnp.bfloat16),
        "tile_rows": touch_ends(jax.random.randint(key_of[5], (N_GROUP, N_BLK, N_GROUP, STEPS, CAP), 0, RT), jax.random.fold_in(key_of[5], 1), 0, RT - 1).astype(jnp.int32),
        "tile_cols": touch_ends(jax.random.randint(key_of[6], (N_GROUP, N_BLK, N_GROUP, STEPS, CAP), 0, CT), jax.random.fold_in(key_of[6], 1), 0, CT - 1).astype(jnp.int32),
        "tile_counts": draw_tile_counts(jax.random.fold_in(key_of[9], 71), 0),
        "negatives": touch_ends(jax.random.randint(key_of[8], (N_GROUP, N_BLK, STEPS, RT, NNEG), 0, CT), jax.random.fold_in(key_of[8], 1), 0, CT - 1).astype(jnp.int32),
    }


LEARNING = 0.1
NEG_WEIGHT = 0.5

def lowered(values):
    return lax.optimization_barrier(values.astype(jnp.bfloat16)).astype(jnp.float32)

def device_gradients(vertex_rows, context_rows, weights, row_ids, col_ids, negative_ids):
    width = vertex_rows.shape[1]
    tile = weights.shape[-1]
    vertex_tiles = vertex_rows.astype(jnp.bfloat16).astype(jnp.float32).reshape(-1, tile, width)
    context_tiles = context_rows.astype(jnp.bfloat16).astype(jnp.float32).reshape(-1, tile, width)
    vertex_pick = jnp.take(vertex_tiles, row_ids, axis=0)
    context_pick = jnp.take(context_tiles, col_ids, axis=0)
    logits = jnp.einsum('nid,njd->nij', vertex_pick, context_pick)
    pos_grad = lowered(weights.astype(jnp.float32) * (jax.nn.sigmoid(logits) - 1.0))
    vertex_terms = jnp.einsum('nij,njd->nid', pos_grad, context_pick)
    context_terms = jnp.einsum('nij,nid->njd', pos_grad, vertex_pick)
    row_hot = (row_ids[:, None] == jnp.arange(vertex_tiles.shape[0])[None, :]).astype(jnp.float32)
    col_hot = (col_ids[:, None] == jnp.arange(context_tiles.shape[0])[None, :]).astype(jnp.float32)
    vertex_grad = jnp.einsum('nr,nid->rid', row_hot, vertex_terms)
    context_grad = jnp.einsum('nc,njd->cjd', col_hot, context_terms)
    neg_pick = jnp.take(context_tiles, negative_ids, axis=0)
    neg_logits = jnp.einsum('rid,rkjd->rkij', vertex_tiles, neg_pick)
    neg_grad = lowered(NEG_WEIGHT * jax.nn.sigmoid(neg_logits))
    vertex_grad = vertex_grad + jnp.einsum('rkij,rkjd->rid', neg_grad, neg_pick)
    neg_terms = jnp.einsum('rkij,rid->rkjd', neg_grad, vertex_tiles)
    neg_hot = (negative_ids[:, :, None] == jnp.arange(context_tiles.shape[0])[None, None, :]).astype(jnp.float32)
    context_grad = context_grad + jnp.einsum('rkc,rkjd->cjd', neg_hot, neg_terms)
    return (vertex_grad.reshape(-1, width), context_grad.reshape(-1, width))

def adagrad(rows, state, grad):
    new_state = state + lax.optimization_barrier(jnp.mean(grad * grad, axis=1))
    return (rows - LEARNING * grad / jnp.sqrt(new_state)[:, None], new_state)

def reference(vertex, vertex_state, context, context_state, tile_weights, tile_rows, tile_cols, tile_counts, negatives):
    groups = N_GROUP
    blocks = N_BLK
    devices = groups * blocks
    vertex_all = vertex.reshape(devices, R_DEV, D)
    vstate_all = vertex_state.reshape(devices, R_DEV)
    context_all = context.reshape(devices, CTX, D)
    cstate_all = context_state.reshape(devices, CTX)
    received = jnp.transpose(tile_weights, (2, 1, 0, 3, 4, 5, 6))
    rows_all = jnp.transpose(tile_rows, (2, 1, 0, 3, 4)).reshape(devices, groups, STEPS, CAP)
    cols_all = jnp.transpose(tile_cols, (2, 1, 0, 3, 4)).reshape(devices, groups, STEPS, CAP)
    counts_all = jnp.transpose(tile_counts, (2, 1, 0, 3))
    valid = jnp.arange(CAP)[None, None, None, None, :] < counts_all[..., None]
    masked = jnp.where(valid[..., None, None], received, jnp.zeros((), jnp.bfloat16))
    masked = masked.reshape(devices, groups, STEPS, CAP, TILE, TILE)
    neg_all = negatives.reshape(devices, STEPS, RT, NNEG)
    for stop_index in range(STEPS):

        def one_device(items):
            vrows, vstate, crows, cstate, weights, row_ids, col_ids, neg_ids = items
            vertex_grad, context_grad = device_gradients(vrows, crows, weights.reshape(-1, TILE, TILE), row_ids.reshape(-1), col_ids.reshape(-1), neg_ids)
            vrows, vstate = adagrad(vrows, vstate, vertex_grad)
            crows, cstate = adagrad(crows, cstate, context_grad)
            return (vrows, vstate, crows, cstate)
        vertex_all, vstate_all, context_all, cstate_all = lax.map(one_device, (vertex_all, vstate_all, context_all, cstate_all, masked[:, :, stop_index], rows_all[:, :, stop_index], cols_all[:, :, stop_index], neg_all[:, stop_index]))
        if stop_index < STEPS - 1:
            context_all = jnp.roll(context_all.reshape(groups, blocks, CTX, D), 1, axis=1).reshape(devices, CTX, D)
            cstate_all = jnp.roll(cstate_all.reshape(groups, blocks, CTX), 1, axis=1).reshape(devices, CTX)
    return (vertex_all.reshape(-1, D), vstate_all.reshape(-1), context_all.reshape(-1, D), cstate_all.reshape(-1))
```

```python
import functools

import jax
import jax.numpy as jnp
from jax import lax
from jax.experimental import pallas as pl
from jax.experimental.pallas import tpu as pltpu
from jax.sharding import PartitionSpec as P

LEARNING = 0.1
TILE = 128
F32 = jnp.float32
BF16 = jnp.bfloat16
NT = (((1,), (1,)), ((), ()))
NN = (((1,), (0,)), ((), ()))
TN = (((0,), (0,)), ((), ()))


def dot(a, b, dims):
    return lax.dot_general(a, b, dims, preferred_element_type=F32)


def eye_mask():
    return lax.broadcasted_iota(jnp.int32, (TILE, TILE), 0) == lax.broadcasted_iota(
        jnp.int32, (TILE, TILE), 1
    )


def to_column(eye, row):
    return jnp.sum(jnp.where(eye, row, 0.0), axis=1, keepdims=True)


def to_row(eye, column):
    return jnp.sum(jnp.where(eye, column, 0.0), axis=0, keepdims=True)


def adagrad(eye, rows, state_row, grad):
    width = grad.shape[1]
    state = to_column(eye, state_row) + jnp.sum(grad * grad, axis=1, keepdims=True) * (1.0 / width)
    return rows - (LEARNING * grad) * lax.rsqrt(state), to_row(eye, state)


def stack_rows(rows, height):
    which = lax.broadcasted_iota(jnp.int32, (height, TILE), 0)
    out = jnp.zeros((height, TILE), F32)
    for t, row in enumerate(rows):
        out = jnp.where(which == t, row, out)
    return out


def context_kernel(first, last, stop, *refs):
    ids_ref, neg_ref, v_ref, *refs = refs
    if first:
        c_ref, cs_ref, *refs = refs
    else:
        msg_ref, *refs = refs
    w_refs, refs = refs[:4], refs[4:]
    p_ref, *outs = refs
    *outs, wsum = outs

    rt = v_ref.shape[0] // TILE
    ctx = p_ref.shape[1]
    ct = ctx // TILE
    cap = w_refs[0].shape[0]

    wsum[...] = jnp.zeros_like(wsum)
    for src in range(4):
        for slot in range(cap):
            pair = ids_ref[src, stop, slot]
            wsum[pair] += w_refs[src][slot].astype(F32)

    if first:
        c_now = c_ref[...]
        c_bf = c_now.astype(BF16)
        states = cs_ref[...]
    else:
        c_bf = msg_ref[:ctx, :]
        c_now = c_bf.astype(F32)
        tail = msg_ref[ctx:, :].astype(F32)
        states = tail[:, :TILE] + tail[:, TILE:]

    for r in range(rt):
        rows = pl.ds(r * TILE, TILE)
        v_tile = v_ref[rows, :].astype(BF16)
        t_val = jnp.tanh(0.5 * dot(v_tile, c_bf, NT))
        for c in range(ct):
            cols = slice(c * TILE, (c + 1) * TILE)
            count = jnp.int32(0)
            for k in range(neg_ref.shape[2]):
                count += (neg_ref[stop, r, k] == c).astype(jnp.int32)
            q = 0.25 * count.astype(F32)
            half = 0.5 * wsum[r * ct + c]
            tt = t_val[:, cols]
            p_ref[rows, cols] = (half * (tt - 1.0) + q * (tt + 1.0)).astype(BF16)

    grad = dot(p_ref[...], v_ref[...].astype(BF16), TN)
    eye = eye_mask()
    new_states = []
    for c in range(ct):
        rows = slice(c * TILE, (c + 1) * TILE)
        new_rows, new_state = adagrad(eye, c_now[rows], states[c : c + 1], grad[rows])
        new_states.append(new_state)
        if last:
            outs[0][rows, :] = new_rows
            outs[1][c : c + 1, :] = new_state
        else:
            outs[0][rows, :] = new_rows.astype(BF16)
    if not last:
        block = stack_rows(new_states, outs[0].shape[0] - ctx)
        hi = block.astype(BF16)
        outs[0][ctx:, :TILE] = hi
        outs[0][ctx:, TILE:] = (block - hi.astype(F32)).astype(BF16)


def vertex_kernel(last, p_ref, c_ref, v_ref, vs_ref, vout_ref, vsout_ref, *more):
    ctx = p_ref.shape[1]
    c_bf = c_ref[:ctx, :].astype(BF16)
    eye = eye_mask()
    for r in range(v_ref.shape[0] // TILE):
        rows = pl.ds(r * TILE, TILE)
        grad = dot(p_ref[rows, :], c_bf, NN)
        new_rows, new_state = adagrad(eye, v_ref[rows, :], vs_ref[r : r + 1, :], grad)
        vout_ref[rows, :] = new_rows
        vsout_ref[r : r + 1, :] = new_state
        if not last:
            more[0][rows, :] = new_rows.astype(BF16)


VM = pl.BlockSpec(memory_space=pltpu.VMEM)
SM = pl.BlockSpec(memory_space=pltpu.SMEM)


def context_call(stop, first, last, ids, neg, v, context, weights):
    rt = v.shape[0] // TILE
    ctx = context[0].shape[0] if first else context[0].shape[0] - 16
    width = v.shape[1]
    pairs = rt * (ctx // TILE)
    if last:
        outs = [((ctx, width), F32), ((ctx // TILE, TILE), F32)]
    else:
        outs = [((ctx + 16, width), BF16)]
    outs = [((v.shape[0], ctx), BF16)] + outs
    args = (ids, neg, v, *context, *weights)
    return pl.pallas_call(
        functools.partial(context_kernel, first, last, stop),
        out_shape=[jax.ShapeDtypeStruct(s, d) for s, d in outs],
        in_specs=[SM, SM] + [VM] * (len(args) - 2),
        out_specs=[VM] * len(outs),
        scratch_shapes=[pltpu.VMEM((pairs + 1, TILE, TILE), F32)],
        compiler_params=pltpu.CompilerParams(vmem_limit_bytes=24 << 20),
        cost_estimate=pl.CostEstimate(
            flops=4 * v.shape[0] * ctx * width, bytes_accessed=4 << 20, transcendentals=v.shape[0] * ctx
        ),
        name="context_%d" % stop,
    )(*args)


def vertex_call(stop, last, p, c, v, vs):
    outs = [(v.shape, F32), (vs.shape, F32)]
    if not last:
        outs.append((v.shape, BF16))
    return pl.pallas_call(
        functools.partial(vertex_kernel, last),
        out_shape=[jax.ShapeDtypeStruct(s, d) for s, d in outs],
        in_specs=[VM] * 4,
        out_specs=[VM] * len(outs),
        compiler_params=pltpu.CompilerParams(vmem_limit_bytes=24 << 20),
        cost_estimate=pl.CostEstimate(
            flops=2 * v.shape[0] * c.shape[0] * v.shape[1], bytes_accessed=4 << 20, transcendentals=v.shape[0]
        ),
        name="vertex_%d" % stop,
    )(p, c, v, vs)


def shifted(value, axis, by):
    peers = lax.axis_size(axis)
    return lax.ppermute(value, axis, [(i, (i + by) % peers) for i in range(peers)])


def swapped(value, by):
    peers = lax.axis_size("group")
    return lax.ppermute(value, "group", [(i, i ^ by) for i in range(peers)])


def body(vertex, vertex_state, context, context_state, tile_weights, tile_rows, tile_cols, tile_counts, negatives):
    weights = tile_weights[0, 0]
    groups, stops, cap = weights.shape[:3]
    rt, ct = vertex.shape[0] // TILE, context.shape[0] // TILE
    me = lax.axis_index("group")

    valid = jnp.arange(cap)[None, None, :] < tile_counts[0, 0][..., None]
    codes = jnp.where(valid, tile_rows[0, 0] * ct + tile_cols[0, 0], rt * ct).astype(jnp.int32)

    def mine(array, by):
        return lax.dynamic_index_in_dim(array, me ^ by, 0, keepdims=False)

    ids = [mine(codes, 0)] + [swapped(mine(codes, by), by) for by in range(1, groups)]
    ids = jnp.stack(ids)
    neg = negatives[0, 0]

    def exchanged(stop):
        out = []
        for by in range(groups):
            piece = lax.dynamic_slice(
                weights, (me ^ by, stop, 0, 0, 0), (1, 1, cap, TILE, TILE)
            ).reshape(cap, TILE, TILE)
            out.append(swapped(piece, by) if by else piece)
        return out

    arrived = [exchanged(stop) for stop in range(stops)]
    v, vs = vertex, vertex_state.reshape(rt, TILE)
    v_bf = vertex
    held = (context, context_state.reshape(ct, TILE))
    for stop in range(stops):
        first, last = stop == 0, stop == stops - 1
        p, *new = context_call(stop, first, last, ids, neg, v_bf, held, arrived[stop])
        if not last:
            sent = shifted(new[0], "blk", 1)
        v, vs, *rest = vertex_call(stop, last, p, held[0], v, vs)
        if not last:
            v_bf = rest[0]
            held = (sent,)
    return v, vs.reshape(-1), new[0], new[1].reshape(-1)


def solution(mesh):
    in_specs = (
        P(("group", "blk"), None),
        P(("group", "blk")),
        P(("group", "blk"), None),
        P(("group", "blk")),
        P("group", "blk", None, None, None, None, None),
        P("group", "blk", None, None, None),
        P("group", "blk", None, None, None),
        P("group", "blk", None, None),
        P("group", "blk", None, None, None),
    )
    out_specs = (
        P(("group", "blk"), None),
        P(("group", "blk")),
        P(("group", "blk"), None),
        P(("group", "blk")),
    )
    return jax.shard_map(body, mesh=mesh, in_specs=in_specs, out_specs=out_specs, check_vma=False)
```

```python
import functools

import jax
import jax.numpy as jnp
from jax import lax
from jax.experimental import pallas as pl
from jax.experimental.pallas import tpu as pltpu
from jax.sharding import PartitionSpec as P

LEARNING = 0.1
TILE = 128
BLOCK = 256
F32 = jnp.float32
BF16 = jnp.bfloat16
NT = (((1,), (1,)), ((), ()))
NN = (((1,), (0,)), ((), ()))
TN = (((0,), (0,)), ((), ()))
VM = pl.BlockSpec(memory_space=pltpu.VMEM)
SM = pl.BlockSpec(memory_space=pltpu.SMEM)
HBM = pl.BlockSpec(memory_space=pltpu.HBM)
FREE = pl.CostEstimate(flops=0, bytes_accessed=0, transcendentals=0)
ROOM = 24 << 20
PACK_ROOM = 60 << 20
ROW_TILES = 8
PAIRS = 32
CHUNKS = 2
TAIL = 16
ID_ROWS = 8


def dot(a, b, dims):
    return lax.dot_general(a, b, dims, preferred_element_type=F32)


def eye_mask():
    return lax.broadcasted_iota(jnp.int32, (TILE, TILE), 0) == lax.broadcasted_iota(
        jnp.int32, (TILE, TILE), 1
    )


def to_column(eye, row):
    return jnp.sum(jnp.where(eye, row, 0.0), axis=1, keepdims=True)


def to_row(eye, column):
    return jnp.sum(jnp.where(eye, column, 0.0), axis=0, keepdims=True)


def adagrad(eye, rows, state_row, grad):
    width = grad.shape[1]
    state = to_column(eye, state_row) + jnp.sum(grad * grad, axis=1, keepdims=True) * (1.0 / width)
    return rows - (LEARNING * grad) * lax.rsqrt(state), to_row(eye, state)


def stack_rows(rows, height):
    which = lax.broadcasted_iota(jnp.int32, (height, TILE), 0)
    out = jnp.zeros((height, TILE), F32)
    for t, row in enumerate(rows):
        out = jnp.where(which == t, row, out)
    return out


def context_kernel(first, last, stop, base, *refs):
    neg_ref, v_ref, w_ref, *refs = refs
    if first:
        c_ref, cs_ref, pt_ref, *outs = refs
        height = pt_ref.shape[0]
        tiles = slice(base, base + height // TILE)
        c_now = c_ref[base * TILE : base * TILE + height, :]
        c_bf = c_now.astype(BF16)
        states = cs_ref[tiles, :]
    else:
        parts = len(refs) - (3 if last else 2)
        msgs, (pt_ref, *outs) = refs[:parts], refs[parts:]
        part = msgs[0].shape[0] - TAIL
        height = part * parts
        c_bf = jnp.concatenate([msg[:part, :] for msg in msgs], axis=0)
        c_now = c_bf.astype(F32)
        tails = [msg[part:, :].astype(F32) for msg in msgs]
        states = jnp.concatenate(
            [(tail[:, :TILE] + tail[:, TILE:])[: part // TILE] for tail in tails], axis=0
        )

    rows_v = v_ref.shape[0]
    rt, ct = rows_v // TILE, height // TILE
    for block in range(rows_v // BLOCK):
        v_block = v_ref[block * BLOCK : (block + 1) * BLOCK, :].astype(BF16)
        t_val = jnp.tanh(0.5 * dot(c_bf, v_block, NT))
        for c in range(ct):
            for k in range(BLOCK // TILE):
                r = block * (BLOCK // TILE) + k
                count = jnp.int32(0)
                for n in range(neg_ref.shape[1]):
                    count += (neg_ref[stop, n, r] == base + c).astype(jnp.int32)
                q = 0.25 * count.astype(F32)
                half = w_ref[(base + c) * rt + r]
                tt = t_val[c * TILE : (c + 1) * TILE, k * TILE : (k + 1) * TILE]
                pt_ref[c * TILE : (c + 1) * TILE, r * TILE : (r + 1) * TILE] = (
                    half * (tt - 1.0) + q * (tt + 1.0)
                ).astype(BF16)

    grad = dot(pt_ref[...], v_ref[...].astype(BF16), NN)
    eye = eye_mask()
    new_states = []
    for c in range(ct):
        rows = slice(c * TILE, (c + 1) * TILE)
        new_rows, new_state = adagrad(eye, c_now[rows], states[c : c + 1], grad[rows])
        new_states.append(new_state)
        if last:
            outs[0][rows, :] = new_rows
            outs[1][c : c + 1, :] = new_state
        else:
            outs[0][rows, :] = new_rows.astype(BF16)
    if not last:
        block = stack_rows(new_states, TAIL)
        hi = block.astype(BF16)
        outs[0][height:, :TILE] = hi
        outs[0][height:, TILE:] = (block - hi.astype(F32)).astype(BF16)


def vertex_kernel(last, n_pt, n_c, *refs):
    pt_refs, c_refs, refs = refs[:n_pt], refs[n_pt : n_pt + n_c], refs[n_pt + n_c :]
    v_ref, vs_ref, vout_ref, vsout_ref, *more = refs
    ctx = sum(ref.shape[0] for ref in pt_refs)
    c_bf = jnp.concatenate([ref[: ctx // n_c, :] for ref in c_refs], axis=0).astype(BF16)
    eye = eye_mask()
    for r in range(v_ref.shape[0] // TILE):
        rows = slice(r * TILE, (r + 1) * TILE)
        pt = jnp.concatenate([ref[:, rows] for ref in pt_refs], axis=0)
        grad = dot(pt, c_bf, TN)
        new_rows, new_state = adagrad(eye, v_ref[rows, :], vs_ref[r : r + 1, :], grad)
        vout_ref[rows, :] = new_rows
        vsout_ref[r : r + 1, :] = new_state
        if not last:
            more[0][rows, :] = new_rows.astype(BF16)


def add_tiles(out_ref, tiles):
    for pair, tile in tiles:
        out_ref[pair] += 0.5 * tile.astype(F32).T


def near_kernel(own_ref, one_ref, near_ref, out_ref):
    out_ref[...] = jnp.zeros_like(out_ref)
    cap = near_ref.shape[0] // 2
    add_tiles(
        out_ref,
        [(ref[slot, 0], near_ref[k * cap + slot]) for k, ref in enumerate((own_ref, one_ref)) for slot in range(cap)],
    )


def first_weights_kernel(own_ref, one_ref, part_ref, two_ref, three_ref, out_ref, ids_ref, scalars, sem):
    msgs = two_ref, three_ref
    cap = (two_ref.shape[0] - TAIL) // TILE
    for at, msg in enumerate(msgs):
        ids_ref[at + 2] = msg[cap * TILE :, :].astype(F32)[:ID_ROWS].astype(jnp.int32)
    copy = pltpu.make_async_copy(ids_ref.at[pl.ds(2, 2)], scalars, sem)
    copy.start()
    ids_ref[0] = own_ref[...]
    ids_ref[1] = one_ref[...]
    copy.wait()
    add_tiles(
        out_ref,
        [
            (scalars[at, slot, 0], msg[slot * TILE : (slot + 1) * TILE, :])
            for at, msg in enumerate(msgs)
            for slot in range(cap)
        ],
    )


def weights_kernel(stop, ids_ref, near_ref, far_ref, out_ref):
    out_ref[...] = jnp.zeros_like(out_ref)
    cap = far_ref.shape[0] // 2
    tiles = [ref[t] for ref in (near_ref, far_ref) for t in range(2 * cap)]
    add_tiles(out_ref, [(ids_ref[at // cap, at % cap, stop], tile) for at, tile in enumerate(tiles)])


def pack_kernel(me_ref, w_ref, rows_ref, cols_ref, counts_ref, *refs):
    groups, _, cap = w_ref.shape[:3]
    outs, (given, counts, ids, sem) = refs[:4], refs[4:]
    msgs = outs[2:]
    me = me_ref[0]
    fetches = [
        pltpu.make_async_copy(rows_ref, given.at[0], sem.at[0]),
        pltpu.make_async_copy(cols_ref, given.at[1], sem.at[1]),
        pltpu.make_async_copy(counts_ref, counts, sem.at[2]),
    ]
    for copy in fetches:
        copy.start()
    copies = [
        pltpu.make_async_copy(
            w_ref.at[me ^ (at + 2), 0, slot], msg.at[pl.ds(slot * TILE, TILE)], sem.at[3 + at * cap + slot]
        )
        for at, msg in enumerate(msgs)
        for slot in range(cap)
    ]
    for copy in copies:
        copy.start()
    ids[...] = jnp.zeros_like(ids)
    for copy in fetches:
        copy.wait()
    stops = counts.shape[1]
    for slot in range(cap):
        code = jnp.where(slot < counts[...], given[1, slot] * ROW_TILES + given[0, slot], PAIRS)
        which = lax.broadcasted_iota(jnp.int32, code.shape, 0)
        for by in range(groups):
            kept = jnp.sum(jnp.where(which == (me ^ by), code, 0), axis=0, keepdims=True)
            ids[by, slot : slot + 1, :stops] = kept
    outs[0][...] = ids[0, :ID_ROWS]
    outs[1][...] = ids[1, :ID_ROWS]
    for at, msg in enumerate(msgs):
        msg[cap * TILE :, :] = ids[at + 2].astype(F32).astype(BF16)
    for copy in copies:
        copy.wait()


def relay_kernel(stop, me_ref, w_ref, sib_ref, after_ref, *refs):
    *out_refs, sem = refs
    me = me_ref[0]
    cap = w_ref.shape[2]
    copies = []
    for n, (dst, by, at) in enumerate(zip(out_refs, (2, 0, 0), (stop, stop, 0))):
        for half, src in enumerate((w_ref, sib_ref)):
            copies.append(
                pltpu.make_async_copy(
                    src.at[me ^ by, at], dst.at[pl.ds(half * cap, cap)], sem.at[2 * n + half]
                )
            )
    for copy in copies:
        copy.start()
    for copy in copies:
        copy.wait()


def params(room=ROOM):
    return pltpu.CompilerParams(vmem_limit_bytes=room)


def context_call(stop, first, last, chunk, neg, v, context, w):
    width = v.shape[1]
    if first:
        height = context[0].shape[0] // CHUNKS
    else:
        height = len(context) * (context[0].shape[0] - TAIL)
    if last:
        outs = [((height, width), F32), ((height // TILE, TILE), F32)]
    else:
        outs = [((height + TAIL, width), BF16)]
    outs = [((height, v.shape[0]), BF16)] + outs
    args = (neg, v, w, *context)
    return pl.pallas_call(
        functools.partial(context_kernel, first, last, stop, chunk * height // TILE),
        out_shape=[jax.ShapeDtypeStruct(s, d) for s, d in outs],
        in_specs=[SM] + [VM] * (len(args) - 1),
        out_specs=[VM] * len(outs),
        compiler_params=params(),
        cost_estimate=FREE,
        name="context_%d_%d" % (stop, chunk),
    )(*args)


def vertex_call(stop, last, pts, cs, v, vs):
    outs = [(v.shape, F32), (vs.shape, F32)]
    if not last:
        outs.append((v.shape, BF16))
    return pl.pallas_call(
        functools.partial(vertex_kernel, last, len(pts), len(cs)),
        out_shape=[jax.ShapeDtypeStruct(s, d) for s, d in outs],
        in_specs=[VM] * (len(pts) + len(cs) + 2),
        out_specs=[VM] * len(outs),
        compiler_params=params(),
        cost_estimate=FREE,
        name="vertex_%d" % stop,
    )(*pts, *cs, v, vs)


def weights_call(stop, ids, near, far):
    return pl.pallas_call(
        functools.partial(weights_kernel, stop),
        out_shape=shape(PAIRS + 1, TILE, TILE, dtype=F32),
        in_specs=[SM] + [VM] * 2,
        out_specs=VM,
        compiler_params=params(),
        cost_estimate=FREE,
        name="weights_%d" % stop,
    )(ids, near, far)


def relay_call(stop, me, weights, sibling, after):
    cap = weights.shape[2]
    count = 3 if stop == 1 else 2
    return pl.pallas_call(
        functools.partial(relay_kernel, stop),
        out_shape=[shape(2 * cap, TILE, TILE)] * count,
        in_specs=[SM, HBM, HBM, HBM],
        out_specs=[VM] * count,
        scratch_shapes=[pltpu.SemaphoreType.DMA((2 * count,))],
        compiler_params=params(),
        cost_estimate=FREE,
        name="relay_%d" % stop,
    )(me, weights, sibling, after)


def shifted(value, axis, by):
    peers = lax.axis_size(axis)
    return lax.ppermute(value, axis, [(i, (i + by) % peers) for i in range(peers)])


def swapped(value, by):
    peers = lax.axis_size("group")
    return lax.ppermute(value, "group", [(i, i ^ by) for i in range(peers)])


def shape(*dims, dtype=BF16):
    return jax.ShapeDtypeStruct(dims, dtype)


def body(vertex, vertex_state, context, context_state, tile_weights, tile_rows, tile_cols, tile_counts, negatives):
    weights = tile_weights[0, 0]
    groups, stops, cap = weights.shape[:3]
    rt, ct = vertex.shape[0] // TILE, context.shape[0] // TILE
    assert (groups, rt, rt * ct) == (4, ROW_TILES, PAIRS)
    me = lax.axis_index("group").astype(jnp.int32).reshape(1)
    neg = jnp.transpose(negatives[0, 0], (0, 2, 1))

    outs = [shape(ID_ROWS, TILE, dtype=jnp.int32)] * 2 + [shape(cap * TILE + TAIL, TILE)] * 2
    own_ids, one_ids, *msgs = pl.pallas_call(
        pack_kernel,
        out_shape=outs,
        in_specs=[SM, HBM, HBM, HBM, HBM],
        out_specs=[VM] * len(outs),
        scratch_shapes=[
            pltpu.VMEM((2, cap, groups, stops), jnp.int32),
            pltpu.VMEM((groups, stops), jnp.int32),
            pltpu.VMEM((groups, TAIL, TILE), jnp.int32),
            pltpu.SemaphoreType.DMA((3 + 2 * cap,)),
        ],
        compiler_params=params(PACK_ROOM),
        cost_estimate=FREE,
        name="pack",
    )(
        me,
        weights,
        jnp.transpose(tile_rows[0, 0], (2, 0, 1)),
        jnp.transpose(tile_cols[0, 0], (2, 0, 1)),
        tile_counts[0, 0],
    )
    later, _ = lax.optimization_barrier((weights, msgs[0]))
    sibling = swapped(later, 1)
    two, three, one_ids = swapped(msgs[0], 2), swapped(msgs[1], 3), swapped(one_ids, 1)

    def relay(stop, after):
        far, *near = relay_call(stop, me, weights, sibling, after)
        return near, swapped(far, 2)

    (near, near_first), far = relay(1, one_ids)
    arrived = {1: ((near,), far)}
    part = pl.pallas_call(
        near_kernel,
        out_shape=shape(PAIRS + 1, TILE, TILE, dtype=F32),
        in_specs=[SM, SM, VM],
        out_specs=VM,
        compiler_params=params(),
        cost_estimate=FREE,
        name="near_0",
    )(own_ids, one_ids, near_first)
    w_sum, ids = pl.pallas_call(
        first_weights_kernel,
        out_shape=[shape(PAIRS + 1, TILE, TILE, dtype=F32), shape(groups, ID_ROWS, TILE, dtype=jnp.int32)],
        in_specs=[VM] * 5,
        out_specs=[VM] * 2,
        scratch_shapes=[pltpu.SMEM((2, ID_ROWS, TILE), jnp.int32), pltpu.SemaphoreType.DMA],
        input_output_aliases={2: 0},
        compiler_params=params(),
        cost_estimate=FREE,
        name="weights_0",
    )(own_ids, one_ids, part, two, three)

    v, vs = vertex, vertex_state.reshape(rt, TILE)
    v_bf = vertex
    full = (context, context_state.reshape(ct, TILE))
    held = None
    for stop in range(stops - 1):
        pts, sent = [], []
        for chunk in range(CHUNKS):
            given = full if stop == 0 else (held[chunk],)
            pt, new = context_call(stop, stop == 0, False, chunk, neg, v_bf, given, w_sum)
            pts.append(pt)
            sent.append(shifted(new, "blk", 1))
        (near,), far = arrived[stop + 1]
        w_sum = weights_call(stop + 1, ids, near, far)
        v, vs, v_bf = vertex_call(stop, False, pts, [context] if stop == 0 else held, v, vs)
        if stop + 2 < stops:
            arrived[stop + 2] = relay(stop + 2, vs)
        held = sent
    pt, c_out, cs_out = context_call(stops - 1, False, True, 0, neg, v_bf, held, w_sum)
    v, vs = vertex_call(stops - 1, True, [pt], held, v, vs)
    return v, vs.reshape(-1), c_out, cs_out.reshape(-1)


def solution(mesh):
    in_specs = (
        P(("group", "blk"), None),
        P(("group", "blk")),
        P(("group", "blk"), None),
        P(("group", "blk")),
        P("group", "blk", None, None, None, None, None),
        P("group", "blk", None, None, None),
        P("group", "blk", None, None, None),
        P("group", "blk", None, None),
        P("group", "blk", None, None, None),
    )
    out_specs = (
        P(("group", "blk"), None),
        P(("group", "blk")),
        P(("group", "blk"), None),
        P(("group", "blk")),
    )
    return jax.shard_map(body, mesh=mesh, in_specs=in_specs, out_specs=out_specs, check_vma=False)
```

```python
import functools

import jax
import jax.numpy as jnp
from jax import lax
from jax.experimental import pallas as pl
from jax.experimental.pallas import tpu as pltpu
from jax.sharding import PartitionSpec as P

LEARNING = 0.1
TILE = 128
BLOCK = 256
F32 = jnp.float32
BF16 = jnp.bfloat16
NT = (((1,), (1,)), ((), ()))
NN = (((1,), (0,)), ((), ()))
TN = (((0,), (0,)), ((), ()))
VM = pl.BlockSpec(memory_space=pltpu.VMEM)
SM = pl.BlockSpec(memory_space=pltpu.SMEM)
HBM = pl.BlockSpec(memory_space=pltpu.HBM)
FREE = pl.CostEstimate(flops=0, bytes_accessed=0, transcendentals=0)
ROOM = 24 << 20
PACK_ROOM = 60 << 20
ROW_TILES = 8
PAIRS = 32
CHUNKS = 2
TAIL = 16
ID_ROWS = 8


def dot(a, b, dims):
    return lax.dot_general(a, b, dims, preferred_element_type=F32)


def eye_mask():
    return lax.broadcasted_iota(jnp.int32, (TILE, TILE), 0) == lax.broadcasted_iota(
        jnp.int32, (TILE, TILE), 1
    )


def to_column(eye, row):
    return jnp.sum(jnp.where(eye, row, 0.0), axis=1, keepdims=True)


def to_row(eye, column):
    return jnp.sum(jnp.where(eye, column, 0.0), axis=0, keepdims=True)


def adagrad(eye, rows, state_row, grad):
    width = grad.shape[1]
    state = to_column(eye, state_row) + jnp.sum(grad * grad, axis=1, keepdims=True) * (1.0 / width)
    return rows - (LEARNING * grad) * lax.rsqrt(state), to_row(eye, state)


def stack_rows(rows, height):
    which = lax.broadcasted_iota(jnp.int32, (height, TILE), 0)
    out = jnp.zeros((height, TILE), F32)
    for t, row in enumerate(rows):
        out = jnp.where(which == t, row, out)
    return out


def unpack_message(msg_ref):
    height = msg_ref.shape[0] - TAIL
    tail = msg_ref[height:, :].astype(F32)
    c_bf = msg_ref[:height, :]
    return c_bf, c_bf.astype(F32), tail[:, :TILE] + tail[:, TILE:]


def update_context(base, c_bf, c_now, states, v_ref, w_ref, q_ref, pt_ref):
    rows_v, height = v_ref.shape[0], c_bf.shape[0]
    rt, ct = rows_v // TILE, height // TILE
    for block in range(rows_v // BLOCK):
        v_block = v_ref[block * BLOCK : (block + 1) * BLOCK, :].astype(BF16)
        t_val = jnp.tanh(0.5 * dot(c_bf, v_block, NT))
        for c in range(ct):
            for k in range(BLOCK // TILE):
                r = block * (BLOCK // TILE) + k
                pair = (base + c) * rt + r
                q = q_ref[pair : pair + 1, :]
                half = w_ref[pair]
                tt = t_val[c * TILE : (c + 1) * TILE, k * TILE : (k + 1) * TILE]
                pt_ref[c * TILE : (c + 1) * TILE, r * TILE : (r + 1) * TILE] = (
                    half * (tt - 1.0) + q * (tt + 1.0)
                ).astype(BF16)

    grad = dot(pt_ref[...], v_ref[...].astype(BF16), NN)
    eye = eye_mask()
    result = []
    for c in range(ct):
        rows = slice(c * TILE, (c + 1) * TILE)
        result.append(adagrad(eye, c_now[rows], states[c : c + 1], grad[rows]))
    return result


def context_kernel(first, last, base, v_ref, w_ref, q_ref, *refs):
    if first:
        c_ref, cs_ref, pt_ref, *outs = refs
        height = pt_ref.shape[0]
        c_now = c_ref[base * TILE : base * TILE + height, :]
        c_bf = c_now.astype(BF16)
        states = cs_ref[base : base + height // TILE, :]
    else:
        msg_ref, pt_ref, *outs = refs
        height = pt_ref.shape[0]
        c_bf, c_now, states = unpack_message(msg_ref)
    result = update_context(base, c_bf, c_now, states, v_ref, w_ref, q_ref, pt_ref)
    for c, (new_rows, new_state) in enumerate(result):
        rows = slice(c * TILE, (c + 1) * TILE)
        outs[0][rows, :] = new_rows if last else new_rows.astype(BF16)
        if last:
            outs[1][c : c + 1, :] = new_state
    if not last:
        block = stack_rows([new_state for _, new_state in result], TAIL)
        hi = block.astype(BF16)
        outs[0][height:, :TILE] = hi
        outs[0][height:, TILE:] = (block - hi.astype(F32)).astype(BF16)


def vertex_kernel(n, first, *refs):
    pt_refs, refs = refs[:n], refs[n:]
    n_c = 1 if first else n
    c_refs, refs = refs[:n_c], refs[n_c:]
    v_ref, vs_ref, vout_ref, vsout_ref, vbf_ref = refs
    ctx = sum(ref.shape[0] for ref in pt_refs)
    c_bf = jnp.concatenate([ref[: ctx // n_c, :] for ref in c_refs], axis=0).astype(BF16)
    eye = eye_mask()
    for r in range(v_ref.shape[0] // TILE):
        rows = slice(r * TILE, (r + 1) * TILE)
        pt = jnp.concatenate([ref[:, rows] for ref in pt_refs], axis=0)
        new_rows, new_state = adagrad(eye, v_ref[rows, :], vs_ref[r : r + 1, :], dot(pt, c_bf, TN))
        vout_ref[rows, :] = new_rows
        vsout_ref[r : r + 1, :] = new_state
        vbf_ref[rows, :] = new_rows.astype(BF16)


def final_kernel(n, v_ref, w_ref, q_ref, *refs):
    msgs, refs = refs[:n], refs[n:]
    done, refs = refs[: 3 * (n - 1)], refs[3 * (n - 1) :]
    v32_ref, vs_ref, *refs = refs
    vout_ref, vsout_ref, cout_ref, csout_ref, *refs = refs
    last_pt, c_new, cs_new, v_new, vs_new, sem = refs
    height = last_pt.shape[0]
    tiles = height // TILE
    rt = v_ref.shape[0] // TILE
    stores = []

    def store(src, dst):
        copy = pltpu.make_async_copy(src, dst, sem.at[len(stores)])
        copy.start()
        stores.append(copy)

    for k in range(n - 1):
        _, rows_ref, state_ref = done[3 * k : 3 * k + 3]
        store(rows_ref, cout_ref.at[pl.ds(k * height, height)])
        cs_new[k * tiles : (k + 1) * tiles, :] = state_ref[...]
    base = (n - 1) * tiles
    result = update_context(base, *unpack_message(msgs[-1]), v_ref, w_ref, q_ref, last_pt)
    for c, (new_rows, new_state) in enumerate(result):
        c_new[c * TILE : (c + 1) * TILE, :] = new_rows
        cs_new[base + c : base + c + 1, :] = new_state
    store(c_new, cout_ref.at[pl.ds((n - 1) * height, height)])
    store(cs_new, csout_ref)
    c_bf = jnp.concatenate([msg[:height, :] for msg in msgs], axis=0)
    pt_refs = [done[3 * k] for k in range(n - 1)] + [last_pt]
    eye = eye_mask()
    for r in range(rt):
        rows = slice(r * TILE, (r + 1) * TILE)
        pt = jnp.concatenate([ref[:, rows] for ref in pt_refs], axis=0)
        new_rows, new_state = adagrad(eye, v32_ref[rows, :], vs_ref[r : r + 1, :], dot(pt, c_bf, TN))
        v_new[rows, :] = new_rows
        vs_new[r : r + 1, :] = new_state
        if r % 2:
            store(v_new.at[pl.ds((r - 1) * TILE, 2 * TILE)], vout_ref.at[pl.ds((r - 1) * TILE, 2 * TILE)])
    store(vs_new, vsout_ref)
    for copy in stores:
        copy.wait()


def fill_counts(stop, neg_ref, q_ref):
    per_stop, rt = neg_ref.shape[1:]
    for pair in range(PAIRS):
        count = jnp.int32(0)
        for n in range(per_stop):
            count += (neg_ref[stop, n, pair % rt] == pair // rt).astype(jnp.int32)
        q_ref[pair : pair + 1, :] = jnp.full((1, TILE), 0.25 * count.astype(F32))


def add_tiles(out_ref, tiles):
    for pair, tile in tiles:
        out_ref[pair] += 0.5 * tile.astype(F32).T


def near_kernel(own_ref, one_ref, neg_ref, near_ref, out_ref, q_ref):
    fill_counts(0, neg_ref, q_ref)
    out_ref[...] = jnp.zeros_like(out_ref)
    cap = near_ref.shape[0] // 2
    add_tiles(
        out_ref,
        [(ref[slot, 0], near_ref[k * cap + slot]) for k, ref in enumerate((own_ref, one_ref)) for slot in range(cap)],
    )


def first_weights_kernel(own_ref, one_ref, part_ref, two_ref, three_ref, out_ref, ids_ref, scalars, sem):
    msgs = two_ref, three_ref
    cap = (two_ref.shape[0] - TAIL) // TILE
    for at, msg in enumerate(msgs):
        ids_ref[at + 2] = msg[cap * TILE :, :].astype(F32)[:ID_ROWS].astype(jnp.int32)
    copy = pltpu.make_async_copy(ids_ref.at[pl.ds(2, 2)], scalars, sem)
    copy.start()
    ids_ref[0] = own_ref[...]
    ids_ref[1] = one_ref[...]
    copy.wait()
    add_tiles(
        out_ref,
        [
            (scalars[at, slot, 0], msg[slot * TILE : (slot + 1) * TILE, :])
            for at, msg in enumerate(msgs)
            for slot in range(cap)
        ],
    )


def weights_kernel(stop, ids_ref, neg_ref, near_ref, far_ref, out_ref, q_ref):
    fill_counts(stop, neg_ref, q_ref)
    out_ref[...] = jnp.zeros_like(out_ref)
    cap = far_ref.shape[0] // 2
    tiles = [ref[t] for ref in (near_ref, far_ref) for t in range(2 * cap)]
    add_tiles(out_ref, [(ids_ref[at // cap, at % cap, stop], tile) for at, tile in enumerate(tiles)])


def pack_kernel(me_ref, w_ref, rows_ref, cols_ref, counts_ref, *refs):
    groups, _, cap = w_ref.shape[:3]
    outs, (given, counts, ids, sem) = refs[:4], refs[4:]
    msgs = outs[2:]
    me = me_ref[0]
    fetches = [
        pltpu.make_async_copy(rows_ref, given.at[0], sem.at[0]),
        pltpu.make_async_copy(cols_ref, given.at[1], sem.at[1]),
        pltpu.make_async_copy(counts_ref, counts, sem.at[2]),
    ]
    for copy in fetches:
        copy.start()
    copies = [
        pltpu.make_async_copy(
            w_ref.at[me ^ (at + 2), 0, slot], msg.at[pl.ds(slot * TILE, TILE)], sem.at[3 + at * cap + slot]
        )
        for at, msg in enumerate(msgs)
        for slot in range(cap)
    ]
    for copy in copies:
        copy.start()
    ids[...] = jnp.zeros_like(ids)
    for copy in fetches:
        copy.wait()
    stops = counts.shape[1]
    for slot in range(cap):
        code = jnp.where(slot < counts[...], given[1, slot] * ROW_TILES + given[0, slot], PAIRS)
        which = lax.broadcasted_iota(jnp.int32, code.shape, 0)
        for by in range(groups):
            kept = jnp.sum(jnp.where(which == (me ^ by), code, 0), axis=0, keepdims=True)
            ids[by, slot : slot + 1, :stops] = kept
    outs[0][...] = ids[0, :ID_ROWS]
    outs[1][...] = ids[1, :ID_ROWS]
    for at, msg in enumerate(msgs):
        msg[cap * TILE :, :] = ids[at + 2].astype(F32).astype(BF16)
    for copy in copies:
        copy.wait()


def relay_kernel(stop, me_ref, w_ref, sib_ref, after_ref, *refs):
    *out_refs, sem = refs
    me = me_ref[0]
    cap = w_ref.shape[2]
    copies = []
    for n, (dst, by, at) in enumerate(zip(out_refs, (2, 0, 0), (stop, stop, 0))):
        for half, src in enumerate((w_ref, sib_ref)):
            copies.append(
                pltpu.make_async_copy(
                    src.at[me ^ by, at], dst.at[pl.ds(half * cap, cap)], sem.at[2 * n + half]
                )
            )
    for copy in copies:
        copy.start()
    for copy in copies:
        copy.wait()


def params(room=ROOM):
    return pltpu.CompilerParams(vmem_limit_bytes=room)


def context_call(stop, first, last, chunk, v, context, w, q):
    width = v.shape[1]
    height = context[0].shape[0] // CHUNKS if first else context[0].shape[0] - TAIL
    if last:
        outs = [shape(height, width, dtype=F32), shape(height // TILE, TILE, dtype=F32)]
    else:
        outs = [shape(height + TAIL, width)]
    outs = [shape(height, v.shape[0])] + outs
    args = (v, w, q, *context)
    return pl.pallas_call(
        functools.partial(context_kernel, first, last, chunk * height // TILE),
        out_shape=outs,
        in_specs=[VM] * len(args),
        out_specs=[VM] * len(outs),
        compiler_params=params(),
        cost_estimate=FREE,
        name="context_%d_%d" % (stop, chunk),
    )(*args)


def vertex_call(stop, pts, cs, v, vs):
    outs = [shape(*v.shape, dtype=F32), shape(*vs.shape, dtype=F32), shape(*v.shape)]
    return pl.pallas_call(
        functools.partial(vertex_kernel, len(pts), len(cs) == 1),
        out_shape=outs,
        in_specs=[VM] * (len(pts) + len(cs) + 2),
        out_specs=[VM] * len(outs),
        compiler_params=params(),
        cost_estimate=FREE,
        name="vertex_%d" % stop,
    )(*pts, *cs, v, vs)


def final_call(v_bf, w, q, msgs, done, v, vs):
    n = len(msgs)
    height, width = msgs[0].shape[0] - TAIL, v.shape[1]
    tiles = n * height // TILE
    args = (v_bf, w, q, *msgs, *done, v, vs)
    return pl.pallas_call(
        functools.partial(final_kernel, n),
        out_shape=[
            shape(*v.shape, dtype=F32),
            shape(*vs.shape, dtype=F32),
            shape(n * height, width, dtype=F32),
            shape(tiles, TILE, dtype=F32),
        ],
        in_specs=[VM] * len(args),
        out_specs=[HBM] * 4,
        scratch_shapes=[
            pltpu.VMEM((height, v.shape[0]), BF16),
            pltpu.VMEM((height, width), F32),
            pltpu.VMEM((tiles, TILE), F32),
            pltpu.VMEM(v.shape, F32),
            pltpu.VMEM(vs.shape, F32),
            pltpu.SemaphoreType.DMA((n + 2 + v.shape[0] // (2 * TILE),)),
        ],
        compiler_params=params(),
        cost_estimate=FREE,
        name="final",
    )(*args)


def weights_call(stop, ids, neg, near, far):
    return pl.pallas_call(
        functools.partial(weights_kernel, stop),
        out_shape=[shape(PAIRS + 1, TILE, TILE, dtype=F32), shape(PAIRS, TILE, dtype=F32)],
        in_specs=[SM] * 2 + [VM] * 2,
        out_specs=[VM] * 2,
        compiler_params=params(),
        cost_estimate=FREE,
        name="weights_%d" % stop,
    )(ids, neg, near, far)


def relay_call(stop, me, weights, sibling, after):
    cap = weights.shape[2]
    count = 3 if stop == 1 else 2
    return pl.pallas_call(
        functools.partial(relay_kernel, stop),
        out_shape=[shape(2 * cap, TILE, TILE)] * count,
        in_specs=[SM, HBM, HBM, HBM],
        out_specs=[VM] * count,
        scratch_shapes=[pltpu.SemaphoreType.DMA((2 * count,))],
        compiler_params=params(),
        cost_estimate=FREE,
        name="relay_%d" % stop,
    )(me, weights, sibling, after)


def shifted(value, axis, by):
    peers = lax.axis_size(axis)
    return lax.ppermute(value, axis, [(i, (i + by) % peers) for i in range(peers)])


def swapped(value, by):
    peers = lax.axis_size("group")
    return lax.ppermute(value, "group", [(i, i ^ by) for i in range(peers)])


def shape(*dims, dtype=BF16):
    return jax.ShapeDtypeStruct(dims, dtype)


def body(vertex, vertex_state, context, context_state, tile_weights, tile_rows, tile_cols, tile_counts, negatives):
    weights = tile_weights[0, 0]
    groups, stops, cap = weights.shape[:3]
    rt, ct = vertex.shape[0] // TILE, context.shape[0] // TILE
    assert (groups, rt, rt * ct) == (4, ROW_TILES, PAIRS)
    me = lax.axis_index("group").astype(jnp.int32).reshape(1)
    neg = jnp.transpose(negatives[0, 0], (0, 2, 1))

    outs = [shape(ID_ROWS, TILE, dtype=jnp.int32)] * 2 + [shape(cap * TILE + TAIL, TILE)] * 2
    own_ids, one_ids, *msgs = pl.pallas_call(
        pack_kernel,
        out_shape=outs,
        in_specs=[SM, HBM, HBM, HBM, HBM],
        out_specs=[VM] * len(outs),
        scratch_shapes=[
            pltpu.VMEM((2, cap, groups, stops), jnp.int32),
            pltpu.VMEM((groups, stops), jnp.int32),
            pltpu.VMEM((groups, TAIL, TILE), jnp.int32),
            pltpu.SemaphoreType.DMA((3 + 2 * cap,)),
        ],
        compiler_params=params(PACK_ROOM),
        cost_estimate=FREE,
        name="pack",
    )(
        me,
        weights,
        jnp.transpose(tile_rows[0, 0], (2, 0, 1)),
        jnp.transpose(tile_cols[0, 0], (2, 0, 1)),
        tile_counts[0, 0],
    )
    later, _ = lax.optimization_barrier((weights, msgs[0]))
    sibling = swapped(later, 1)
    two, three, one_ids = swapped(msgs[0], 2), swapped(msgs[1], 3), swapped(one_ids, 1)

    def relay(stop, after):
        far, *near = relay_call(stop, me, weights, sibling, after)
        return near, swapped(far, 2)

    (near, near_first), far = relay(1, one_ids)
    arrived = {1: ((near,), far)}
    part, q = pl.pallas_call(
        near_kernel,
        out_shape=[shape(PAIRS + 1, TILE, TILE, dtype=F32), shape(PAIRS, TILE, dtype=F32)],
        in_specs=[SM, SM, SM, VM],
        out_specs=[VM] * 2,
        compiler_params=params(),
        cost_estimate=FREE,
        name="near_0",
    )(own_ids, one_ids, neg, near_first)
    w_sum, ids = pl.pallas_call(
        first_weights_kernel,
        out_shape=[shape(PAIRS + 1, TILE, TILE, dtype=F32), shape(groups, ID_ROWS, TILE, dtype=jnp.int32)],
        in_specs=[VM] * 5,
        out_specs=[VM] * 2,
        scratch_shapes=[pltpu.SMEM((2, ID_ROWS, TILE), jnp.int32), pltpu.SemaphoreType.DMA],
        input_output_aliases={2: 0},
        compiler_params=params(),
        cost_estimate=FREE,
        name="weights_0",
    )(own_ids, one_ids, part, two, three)

    v, vs = vertex, vertex_state.reshape(rt, TILE)
    v_bf = vertex
    full = (context, context_state.reshape(ct, TILE))
    held = None
    for stop in range(stops - 1):
        pts, sent = [], []
        for chunk in range(CHUNKS):
            given = full if stop == 0 else (held[chunk],)
            pt, new = context_call(stop, stop == 0, False, chunk, v_bf, given, w_sum, q)
            pts.append(pt)
            sent.append(shifted(new, "blk", 1))
        (near,), far = arrived[stop + 1]
        w_sum, q = weights_call(stop + 1, ids, neg, near, far)
        v, vs, v_bf = vertex_call(stop, pts, [context] if stop == 0 else held, v, vs)
        if stop + 2 < stops:
            arrived[stop + 2] = relay(stop + 2, vs)
        held = sent
    done = []
    for chunk in range(CHUNKS - 1):
        done += context_call(stops - 1, False, True, chunk, v_bf, (held[chunk],), w_sum, q)
    v, vs, c_out, cs_out = final_call(v_bf, w_sum, q, held, done, v, vs)
    return v, vs.reshape(-1), c_out, cs_out.reshape(-1)


def solution(mesh):
    in_specs = (
        P(("group", "blk"), None),
        P(("group", "blk")),
        P(("group", "blk"), None),
        P(("group", "blk")),
        P("group", "blk", None, None, None, None, None),
        P("group", "blk", None, None, None),
        P("group", "blk", None, None, None),
        P("group", "blk", None, None),
        P("group", "blk", None, None, None),
    )
    out_specs = (
        P(("group", "blk"), None),
        P(("group", "blk")),
        P(("group", "blk"), None),
        P(("group", "blk")),
    )
    return jax.shard_map(body, mesh=mesh, in_specs=in_specs, out_specs=out_specs, check_vma=False)
```

```python
import functools

import jax
import jax.numpy as jnp
from jax import lax
from jax.experimental import pallas as pl
from jax.experimental.pallas import tpu as pltpu
from jax.sharding import PartitionSpec as P

LEARNING = 0.1
TILE = 128
BLOCK = 256
F32 = jnp.float32
BF16 = jnp.bfloat16
NT = (((1,), (1,)), ((), ()))
NN = (((1,), (0,)), ((), ()))
TN = (((0,), (0,)), ((), ()))
VM = pl.BlockSpec(memory_space=pltpu.VMEM)
SM = pl.BlockSpec(memory_space=pltpu.SMEM)
HBM = pl.BlockSpec(memory_space=pltpu.HBM)
FREE = pl.CostEstimate(flops=0, bytes_accessed=0, transcendentals=0)
ROOM = 24 << 20
PACK_ROOM = 60 << 20
ROW_TILES = 8
PAIRS = 32
CHUNKS = 2
TAIL = 16
ID_ROWS = 8


def dot(a, b, dims):
    return lax.dot_general(a, b, dims, preferred_element_type=F32)


def eye_mask():
    return lax.broadcasted_iota(jnp.int32, (TILE, TILE), 0) == lax.broadcasted_iota(
        jnp.int32, (TILE, TILE), 1
    )


def to_column(eye, row):
    return jnp.sum(jnp.where(eye, row, 0.0), axis=1, keepdims=True)


def to_row(eye, column):
    return jnp.sum(jnp.where(eye, column, 0.0), axis=0, keepdims=True)


def adagrad(eye, rows, state_row, grad):
    width = grad.shape[1]
    state = to_column(eye, state_row) + jnp.sum(grad * grad, axis=1, keepdims=True) * (1.0 / width)
    return rows - (LEARNING * grad) * lax.rsqrt(state), to_row(eye, state)


def stack_rows(rows, height):
    which = lax.broadcasted_iota(jnp.int32, (height, TILE), 0)
    out = jnp.zeros((height, TILE), F32)
    for t, row in enumerate(rows):
        out = jnp.where(which == t, row, out)
    return out


def unpack_message(msg_ref):
    height = msg_ref.shape[0] - TAIL
    tail = msg_ref[height:, :].astype(F32)
    c_bf = msg_ref[:height, :]
    return c_bf, c_bf.astype(F32), tail[:, :TILE] + tail[:, TILE:]


def update_context(base, c_bf, c_now, states, v_ref, w_ref, q_ref, pt_ref):
    rows_v, height = v_ref.shape[0], c_bf.shape[0]
    rt, ct = rows_v // TILE, height // TILE
    c_half = c_bf * jnp.asarray(0.5, BF16)
    for block in range(rows_v // BLOCK):
        v_block = v_ref[block * BLOCK : (block + 1) * BLOCK, :].astype(BF16)
        t_val = jnp.tanh(dot(c_half, v_block, NT))
        for c in range(ct):
            for k in range(BLOCK // TILE):
                r = block * (BLOCK // TILE) + k
                pair = (base + c) * rt + r
                both = 2.0 * q_ref[pair : pair + 1, :]
                tt = t_val[c * TILE : (c + 1) * TILE, k * TILE : (k + 1) * TILE]
                pt_ref[c * TILE : (c + 1) * TILE, r * TILE : (r + 1) * TILE] = (
                    w_ref[pair] * (tt - 1.0) + both
                ).astype(BF16)

    grad = dot(pt_ref[...], v_ref[...].astype(BF16), NN)
    eye = eye_mask()
    result = []
    for c in range(ct):
        rows = slice(c * TILE, (c + 1) * TILE)
        result.append(adagrad(eye, c_now[rows], states[c : c + 1], grad[rows]))
    return result


def context_kernel(first, last, base, v_ref, w_ref, q_ref, *refs):
    if first:
        c_ref, cs_ref, pt_ref, *outs = refs
        height = pt_ref.shape[0]
        c_now = c_ref[base * TILE : base * TILE + height, :]
        c_bf = c_now.astype(BF16)
        states = cs_ref[base : base + height // TILE, :]
    else:
        msg_ref, pt_ref, *outs = refs
        height = pt_ref.shape[0]
        c_bf, c_now, states = unpack_message(msg_ref)
    result = update_context(base, c_bf, c_now, states, v_ref, w_ref, q_ref, pt_ref)
    for c, (new_rows, new_state) in enumerate(result):
        rows = slice(c * TILE, (c + 1) * TILE)
        outs[0][rows, :] = new_rows if last else new_rows.astype(BF16)
        if last:
            outs[1][c : c + 1, :] = new_state
    if not last:
        block = stack_rows([new_state for _, new_state in result], TAIL)
        hi = block.astype(BF16)
        outs[0][height:, :TILE] = hi
        outs[0][height:, TILE:] = (block - hi.astype(F32)).astype(BF16)


def vertex_kernel(n, first, *refs):
    pt_refs, refs = refs[:n], refs[n:]
    n_c = 1 if first else n
    c_refs, refs = refs[:n_c], refs[n_c:]
    v_ref, vs_ref, vout_ref, vsout_ref, vbf_ref = refs
    ctx = sum(ref.shape[0] for ref in pt_refs)
    c_bf = jnp.concatenate([ref[: ctx // n_c, :] for ref in c_refs], axis=0).astype(BF16)
    eye = eye_mask()
    for r in range(v_ref.shape[0] // TILE):
        rows = slice(r * TILE, (r + 1) * TILE)
        pt = jnp.concatenate([ref[:, rows] for ref in pt_refs], axis=0)
        new_rows, new_state = adagrad(eye, v_ref[rows, :], vs_ref[r : r + 1, :], dot(pt, c_bf, TN))
        vout_ref[rows, :] = new_rows
        vsout_ref[r : r + 1, :] = new_state
        vbf_ref[rows, :] = new_rows.astype(BF16)


def final_kernel(n, v_ref, w_ref, q_ref, *refs):
    msgs, refs = refs[:n], refs[n:]
    done, refs = refs[: 3 * (n - 1)], refs[3 * (n - 1) :]
    v32_ref, vs_ref, *refs = refs
    vout_ref, vsout_ref, cout_ref, csout_ref, *refs = refs
    last_pt, c_new, cs_new, v_new, vs_new, sem = refs
    height = last_pt.shape[0]
    tiles = height // TILE
    rt = v_ref.shape[0] // TILE
    stores = []

    def store(src, dst):
        copy = pltpu.make_async_copy(src, dst, sem.at[len(stores)])
        copy.start()
        stores.append(copy)

    for k in range(n - 1):
        _, rows_ref, state_ref = done[3 * k : 3 * k + 3]
        store(rows_ref, cout_ref.at[pl.ds(k * height, height)])
        cs_new[k * tiles : (k + 1) * tiles, :] = state_ref[...]
    base = (n - 1) * tiles
    result = update_context(base, *unpack_message(msgs[-1]), v_ref, w_ref, q_ref, last_pt)
    for c, (new_rows, new_state) in enumerate(result):
        c_new[c * TILE : (c + 1) * TILE, :] = new_rows
        cs_new[base + c : base + c + 1, :] = new_state
    store(c_new, cout_ref.at[pl.ds((n - 1) * height, height)])
    store(cs_new, csout_ref)
    c_bf = jnp.concatenate([msg[:height, :] for msg in msgs], axis=0)
    pt_refs = [done[3 * k] for k in range(n - 1)] + [last_pt]
    eye = eye_mask()
    for r in range(rt):
        rows = slice(r * TILE, (r + 1) * TILE)
        pt = jnp.concatenate([ref[:, rows] for ref in pt_refs], axis=0)
        new_rows, new_state = adagrad(eye, v32_ref[rows, :], vs_ref[r : r + 1, :], dot(pt, c_bf, TN))
        v_new[rows, :] = new_rows
        vs_new[r : r + 1, :] = new_state
        if r % 2:
            store(v_new.at[pl.ds((r - 1) * TILE, 2 * TILE)], vout_ref.at[pl.ds((r - 1) * TILE, 2 * TILE)])
    store(vs_new, vsout_ref)
    for copy in stores:
        copy.wait()


def fill_counts(stop, neg_ref, out_ref, q_ref):
    per_stop, rt = neg_ref.shape[1:]
    for pair in range(PAIRS):
        count = jnp.int32(0)
        for n in range(per_stop):
            count += (neg_ref[stop, n, pair % rt] == pair // rt).astype(jnp.int32)
        value = 0.25 * count.astype(F32)
        q_ref[pair : pair + 1, :] = jnp.full((1, TILE), value)
        out_ref[pair] = jnp.full((TILE, TILE), value)


def add_tiles(out_ref, tiles):
    for pair, tile in tiles:
        out_ref[pair] += 0.5 * tile.astype(F32).T


def near_kernel(own_ref, one_ref, neg_ref, near_ref, out_ref, q_ref):
    fill_counts(0, neg_ref, out_ref, q_ref)
    cap = near_ref.shape[0] // 2
    add_tiles(
        out_ref,
        [(ref[slot, 0], near_ref[k * cap + slot]) for k, ref in enumerate((own_ref, one_ref)) for slot in range(cap)],
    )


def first_weights_kernel(own_ref, one_ref, part_ref, two_ref, three_ref, out_ref, ids_ref, scalars, sem):
    msgs = two_ref, three_ref
    cap = (two_ref.shape[0] - TAIL) // TILE
    for at, msg in enumerate(msgs):
        ids_ref[at + 2] = msg[cap * TILE :, :].astype(F32)[:ID_ROWS].astype(jnp.int32)
    copy = pltpu.make_async_copy(ids_ref.at[pl.ds(2, 2)], scalars, sem)
    copy.start()
    ids_ref[0] = own_ref[...]
    ids_ref[1] = one_ref[...]
    copy.wait()
    add_tiles(
        out_ref,
        [
            (scalars[at, slot, 0], msg[slot * TILE : (slot + 1) * TILE, :])
            for at, msg in enumerate(msgs)
            for slot in range(cap)
        ],
    )


def weights_kernel(stop, ids_ref, neg_ref, near_ref, far_ref, out_ref, q_ref):
    fill_counts(stop, neg_ref, out_ref, q_ref)
    cap = far_ref.shape[0] // 2
    tiles = [ref[t] for ref in (near_ref, far_ref) for t in range(2 * cap)]
    add_tiles(out_ref, [(ids_ref[at // cap, at % cap, stop], tile) for at, tile in enumerate(tiles)])


def pack_kernel(me_ref, w_ref, rows_ref, cols_ref, counts_ref, *refs):
    groups, _, cap = w_ref.shape[:3]
    outs, (given, counts, ids, sem) = refs[:4], refs[4:]
    msgs = outs[2:]
    me = me_ref[0]
    fetches = [
        pltpu.make_async_copy(rows_ref, given.at[0], sem.at[0]),
        pltpu.make_async_copy(cols_ref, given.at[1], sem.at[1]),
        pltpu.make_async_copy(counts_ref, counts, sem.at[2]),
    ]
    for copy in fetches:
        copy.start()
    copies = [
        pltpu.make_async_copy(
            w_ref.at[me ^ (at + 2), 0, slot], msg.at[pl.ds(slot * TILE, TILE)], sem.at[3 + at * cap + slot]
        )
        for at, msg in enumerate(msgs)
        for slot in range(cap)
    ]
    for copy in copies:
        copy.start()
    ids[...] = jnp.zeros_like(ids)
    for copy in fetches:
        copy.wait()
    stops = counts.shape[1]
    for slot in range(cap):
        code = jnp.where(slot < counts[...], given[1, slot] * ROW_TILES + given[0, slot], PAIRS)
        which = lax.broadcasted_iota(jnp.int32, code.shape, 0)
        for by in range(groups):
            kept = jnp.sum(jnp.where(which == (me ^ by), code, 0), axis=0, keepdims=True)
            ids[by, slot : slot + 1, :stops] = kept
    outs[0][...] = ids[0, :ID_ROWS]
    outs[1][...] = ids[1, :ID_ROWS]
    for at, msg in enumerate(msgs):
        msg[cap * TILE :, :] = ids[at + 2].astype(F32).astype(BF16)
    for copy in copies:
        copy.wait()


def relay_kernel(wanted, me_ref, w_ref, sib_ref, after_ref, *refs):
    *out_refs, sem = refs
    me = me_ref[0]
    cap = w_ref.shape[2]
    copies = []
    for n, (dst, (by, stop)) in enumerate(zip(out_refs, wanted)):
        for half, src in enumerate((w_ref, sib_ref)):
            copies.append(
                pltpu.make_async_copy(
                    src.at[me ^ by, stop], dst.at[pl.ds(half * cap, cap)], sem.at[2 * n + half]
                )
            )
    for copy in copies:
        copy.start()
    for copy in copies:
        copy.wait()


def params(room=ROOM):
    return pltpu.CompilerParams(vmem_limit_bytes=room)


def context_call(stop, first, last, chunk, v, context, w, q):
    width = v.shape[1]
    height = context[0].shape[0] // CHUNKS if first else context[0].shape[0] - TAIL
    if last:
        outs = [shape(height, width, dtype=F32), shape(height // TILE, TILE, dtype=F32)]
    else:
        outs = [shape(height + TAIL, width)]
    outs = [shape(height, v.shape[0])] + outs
    args = (v, w, q, *context)
    return pl.pallas_call(
        functools.partial(context_kernel, first, last, chunk * height // TILE),
        out_shape=outs,
        in_specs=[VM] * len(args),
        out_specs=[VM] * len(outs),
        compiler_params=params(),
        cost_estimate=FREE,
        name="context_%d_%d" % (stop, chunk),
    )(*args)


def vertex_call(stop, pts, cs, v, vs):
    outs = [shape(*v.shape, dtype=F32), shape(*vs.shape, dtype=F32), shape(*v.shape)]
    return pl.pallas_call(
        functools.partial(vertex_kernel, len(pts), len(cs) == 1),
        out_shape=outs,
        in_specs=[VM] * (len(pts) + len(cs) + 2),
        out_specs=[VM] * len(outs),
        compiler_params=params(),
        cost_estimate=FREE,
        name="vertex_%d" % stop,
    )(*pts, *cs, v, vs)


def final_call(v_bf, w, q, msgs, done, v, vs):
    n = len(msgs)
    height, width = msgs[0].shape[0] - TAIL, v.shape[1]
    tiles = n * height // TILE
    args = (v_bf, w, q, *msgs, *done, v, vs)
    return pl.pallas_call(
        functools.partial(final_kernel, n),
        out_shape=[
            shape(*v.shape, dtype=F32),
            shape(*vs.shape, dtype=F32),
            shape(n * height, width, dtype=F32),
            shape(tiles, TILE, dtype=F32),
        ],
        in_specs=[VM] * len(args),
        out_specs=[HBM] * 4,
        scratch_shapes=[
            pltpu.VMEM((height, v.shape[0]), BF16),
            pltpu.VMEM((height, width), F32),
            pltpu.VMEM((tiles, TILE), F32),
            pltpu.VMEM(v.shape, F32),
            pltpu.VMEM(vs.shape, F32),
            pltpu.SemaphoreType.DMA((n + 2 + v.shape[0] // (2 * TILE),)),
        ],
        compiler_params=params(),
        cost_estimate=FREE,
        name="final",
    )(*args)


def weights_call(stop, ids, neg, near, far):
    return pl.pallas_call(
        functools.partial(weights_kernel, stop),
        out_shape=[shape(PAIRS + 1, TILE, TILE, dtype=F32), shape(PAIRS, TILE, dtype=F32)],
        in_specs=[SM] * 2 + [VM] * 2,
        out_specs=[VM] * 2,
        compiler_params=params(),
        cost_estimate=FREE,
        name="weights_%d" % stop,
    )(ids, neg, near, far)


def relay_call(wanted, me, weights, sibling, after):
    cap = weights.shape[2]
    return pl.pallas_call(
        functools.partial(relay_kernel, wanted),
        out_shape=[shape(2 * cap, TILE, TILE)] * len(wanted),
        in_specs=[SM, HBM, HBM, HBM],
        out_specs=[VM] * len(wanted),
        scratch_shapes=[pltpu.SemaphoreType.DMA((2 * len(wanted),))],
        compiler_params=params(),
        cost_estimate=FREE,
        name="relay_%d" % wanted[0][1],
    )(me, weights, sibling, after)


def shifted(value, axis, by):
    peers = lax.axis_size(axis)
    return lax.ppermute(value, axis, [(i, (i + by) % peers) for i in range(peers)])


def swapped(value, by):
    peers = lax.axis_size("group")
    return lax.ppermute(value, "group", [(i, i ^ by) for i in range(peers)])


def shape(*dims, dtype=BF16):
    return jax.ShapeDtypeStruct(dims, dtype)


def body(vertex, vertex_state, context, context_state, tile_weights, tile_rows, tile_cols, tile_counts, negatives):
    weights = tile_weights[0, 0]
    groups, stops, cap = weights.shape[:3]
    rt, ct = vertex.shape[0] // TILE, context.shape[0] // TILE
    assert (groups, rt, rt * ct) == (4, ROW_TILES, PAIRS)
    me = lax.axis_index("group").astype(jnp.int32).reshape(1)
    neg = jnp.transpose(negatives[0, 0], (0, 2, 1))

    outs = [shape(ID_ROWS, TILE, dtype=jnp.int32)] * 2 + [shape(cap * TILE + TAIL, TILE)] * 2
    own_ids, one_ids, *msgs = pl.pallas_call(
        pack_kernel,
        out_shape=outs,
        in_specs=[SM, HBM, HBM, HBM, HBM],
        out_specs=[VM] * len(outs),
        scratch_shapes=[
            pltpu.VMEM((2, cap, groups, stops), jnp.int32),
            pltpu.VMEM((groups, stops), jnp.int32),
            pltpu.VMEM((groups, TAIL, TILE), jnp.int32),
            pltpu.SemaphoreType.DMA((3 + 2 * cap,)),
        ],
        compiler_params=params(PACK_ROOM),
        cost_estimate=FREE,
        name="pack",
    )(
        me,
        weights,
        jnp.transpose(tile_rows[0, 0], (2, 0, 1)),
        jnp.transpose(tile_cols[0, 0], (2, 0, 1)),
        tile_counts[0, 0],
    )
    later, _ = lax.optimization_barrier((weights, msgs[0]))
    sibling = swapped(later, 1)
    two, three, one_ids = swapped(msgs[0], 2), swapped(msgs[1], 3), swapped(one_ids, 1)

    far, near, near_first = relay_call(((2, 1), (0, 1), (0, 0)), me, weights, sibling, one_ids)
    arrived = {1: (near, swapped(far, 2))}
    part, q = pl.pallas_call(
        near_kernel,
        out_shape=[shape(PAIRS + 1, TILE, TILE, dtype=F32), shape(PAIRS, TILE, dtype=F32)],
        in_specs=[SM, SM, SM, VM],
        out_specs=[VM] * 2,
        compiler_params=params(),
        cost_estimate=FREE,
        name="near_0",
    )(own_ids, one_ids, neg, near_first)
    w_sum, ids = pl.pallas_call(
        first_weights_kernel,
        out_shape=[shape(PAIRS + 1, TILE, TILE, dtype=F32), shape(groups, ID_ROWS, TILE, dtype=jnp.int32)],
        in_specs=[VM] * 5,
        out_specs=[VM] * 2,
        scratch_shapes=[pltpu.SMEM((2, ID_ROWS, TILE), jnp.int32), pltpu.SemaphoreType.DMA],
        input_output_aliases={2: 0},
        compiler_params=params(),
        cost_estimate=FREE,
        name="weights_0",
    )(own_ids, one_ids, part, two, three)

    v, vs = vertex, vertex_state.reshape(rt, TILE)
    v_bf = vertex
    full = (context, context_state.reshape(ct, TILE))
    held = None
    for stop in range(stops - 1):
        pts, sent = [], []
        for chunk in range(CHUNKS):
            given = full if stop == 0 else (held[chunk],)
            pt, new = context_call(stop, stop == 0, False, chunk, v_bf, given, w_sum, q)
            pts.append(pt)
            sent.append(shifted(new, "blk", 1))
        w_sum, q = weights_call(stop + 1, ids, neg, *arrived[stop + 1])
        v, vs, v_bf = vertex_call(stop, pts, [context] if stop == 0 else held, v, vs)
        if stop + 2 < stops:
            if stop == 0:
                wanted = tuple((by, later) for later in range(2, stops) for by in (2, 0))
                pieces = relay_call(wanted, me, weights, sibling, vs)
            far, _ = lax.optimization_barrier((pieces[2 * stop], vs))
            arrived[stop + 2] = (pieces[2 * stop + 1], swapped(far, 2))
        held = sent
    done = []
    for chunk in range(CHUNKS - 1):
        done += context_call(stops - 1, False, True, chunk, v_bf, (held[chunk],), w_sum, q)
    v, vs, c_out, cs_out = final_call(v_bf, w_sum, q, held, done, v, vs)
    return v, vs.reshape(-1), c_out, cs_out.reshape(-1)


def solution(mesh):
    in_specs = (
        P(("group", "blk"), None),
        P(("group", "blk")),
        P(("group", "blk"), None),
        P(("group", "blk")),
        P("group", "blk", None, None, None, None, None),
        P("group", "blk", None, None, None),
        P("group", "blk", None, None, None),
        P("group", "blk", None, None),
        P("group", "blk", None, None, None),
    )
    out_specs = (
        P(("group", "blk"), None),
        P(("group", "blk")),
        P(("group", "blk"), None),
        P(("group", "blk")),
    )
    return jax.shard_map(body, mesh=mesh, in_specs=in_specs, out_specs=out_specs, check_vma=False)
```

```python
import functools

import jax
import jax.numpy as jnp
from jax import lax
from jax.experimental import pallas as pl
from jax.experimental.pallas import tpu as pltpu
from jax.sharding import PartitionSpec as P

LEARNING = 0.1
TILE = 128
BLOCK = 256
F32 = jnp.float32
BF16 = jnp.bfloat16
NT = (((1,), (1,)), ((), ()))
NN = (((1,), (0,)), ((), ()))
TN = (((0,), (0,)), ((), ()))
VM = pl.BlockSpec(memory_space=pltpu.VMEM)
SM = pl.BlockSpec(memory_space=pltpu.SMEM)
HBM = pl.BlockSpec(memory_space=pltpu.HBM)
FREE = pl.CostEstimate(flops=0, bytes_accessed=0, transcendentals=0)
ROOM = 24 << 20
PACK_ROOM = 60 << 20
ROW_TILES = 8
PAIRS = 32
CHUNKS = 2
TAIL = 16
ID_ROWS = 8


def dot(a, b, dims):
    return lax.dot_general(a, b, dims, preferred_element_type=F32)


def eye_mask():
    return lax.broadcasted_iota(jnp.int32, (TILE, TILE), 0) == lax.broadcasted_iota(
        jnp.int32, (TILE, TILE), 1
    )


def to_column(eye, row):
    return jnp.sum(jnp.where(eye, row, 0.0), axis=1, keepdims=True)


def to_row(eye, column):
    return jnp.sum(jnp.where(eye, column, 0.0), axis=0, keepdims=True)


def adagrad(eye, rows, state_row, grad):
    width = grad.shape[1]
    state = to_column(eye, state_row) + jnp.sum(grad * grad, axis=1, keepdims=True) * (1.0 / width)
    return rows - (LEARNING * grad) * lax.rsqrt(state), to_row(eye, state)


def stack_rows(rows, height):
    which = lax.broadcasted_iota(jnp.int32, (height, TILE), 0)
    out = jnp.zeros((height, TILE), F32)
    for t, row in enumerate(rows):
        out = jnp.where(which == t, row, out)
    return out


def unpack_message(msg_ref):
    height = msg_ref.shape[0] - TAIL
    tail = msg_ref[height:, :].astype(F32)
    c_bf = msg_ref[:height, :]
    return c_bf, c_bf.astype(F32), tail[:, :TILE] + tail[:, TILE:]


def update_context(base, c_bf, c_now, states, v_ref, w_ref, q_ref, pt_ref):
    rows_v, height = v_ref.shape[0], c_bf.shape[0]
    rt, ct = rows_v // TILE, height // TILE
    c_half = c_bf * jnp.asarray(0.5, BF16)
    for block in range(rows_v // BLOCK):
        v_block = v_ref[block * BLOCK : (block + 1) * BLOCK, :].astype(BF16)
        t_val = jnp.tanh(dot(c_half, v_block, NT))
        for c in range(ct):
            for k in range(BLOCK // TILE):
                r = block * (BLOCK // TILE) + k
                pair = (base + c) * rt + r
                both = 2.0 * q_ref[pair : pair + 1, :]
                tt = t_val[c * TILE : (c + 1) * TILE, k * TILE : (k + 1) * TILE]
                pt_ref[c * TILE : (c + 1) * TILE, r * TILE : (r + 1) * TILE] = (
                    w_ref[pair] * (tt - 1.0) + both
                ).astype(BF16)

    grad = dot(pt_ref[...], v_ref[...].astype(BF16), NN)
    eye = eye_mask()
    result = []
    for c in range(ct):
        rows = slice(c * TILE, (c + 1) * TILE)
        result.append(adagrad(eye, c_now[rows], states[c : c + 1], grad[rows]))
    return result


def context_kernel(first, last, base, v_ref, w_ref, q_ref, *refs):
    if first:
        c_ref, cs_ref, pt_ref, *outs = refs
        height = pt_ref.shape[0]
        c_now = c_ref[base * TILE : base * TILE + height, :]
        c_bf = c_now.astype(BF16)
        states = cs_ref[base : base + height // TILE, :]
    else:
        msg_ref, pt_ref, *outs = refs
        height = pt_ref.shape[0]
        c_bf, c_now, states = unpack_message(msg_ref)
    result = update_context(base, c_bf, c_now, states, v_ref, w_ref, q_ref, pt_ref)
    for c, (new_rows, new_state) in enumerate(result):
        rows = slice(c * TILE, (c + 1) * TILE)
        outs[0][rows, :] = new_rows if last else new_rows.astype(BF16)
        if last:
            outs[1][c : c + 1, :] = new_state
    if not last:
        block = stack_rows([new_state for _, new_state in result], TAIL)
        hi = block.astype(BF16)
        outs[0][height:, :TILE] = hi
        outs[0][height:, TILE:] = (block - hi.astype(F32)).astype(BF16)


def vertex_kernel(n, first, *refs):
    pt_refs, refs = refs[:n], refs[n:]
    n_c = 1 if first else n
    c_refs, refs = refs[:n_c], refs[n_c:]
    v_ref, vs_ref, vout_ref, vsout_ref, vbf_ref = refs
    ctx = sum(ref.shape[0] for ref in pt_refs)
    c_bf = jnp.concatenate([ref[: ctx // n_c, :] for ref in c_refs], axis=0).astype(BF16)
    eye = eye_mask()
    for r in range(v_ref.shape[0] // TILE):
        rows = slice(r * TILE, (r + 1) * TILE)
        pt = jnp.concatenate([ref[:, rows] for ref in pt_refs], axis=0)
        new_rows, new_state = adagrad(eye, v_ref[rows, :], vs_ref[r : r + 1, :], dot(pt, c_bf, TN))
        vout_ref[rows, :] = new_rows
        vsout_ref[r : r + 1, :] = new_state
        vbf_ref[rows, :] = new_rows.astype(BF16)


def final_kernel(n, v_ref, w_ref, q_ref, *refs):
    msgs, refs = refs[:n], refs[n:]
    done, refs = refs[: 3 * (n - 1)], refs[3 * (n - 1) :]
    v32_ref, vs_ref, *refs = refs
    vout_ref, vsout_ref, cout_ref, csout_ref, *refs = refs
    last_pt, c_new, cs_new, v_new, vs_new, sem = refs
    height = last_pt.shape[0]
    tiles = height // TILE
    rt = v_ref.shape[0] // TILE
    stores = []

    def store(src, dst):
        copy = pltpu.make_async_copy(src, dst, sem.at[len(stores)])
        copy.start()
        stores.append(copy)

    for k in range(n - 1):
        _, rows_ref, state_ref = done[3 * k : 3 * k + 3]
        store(rows_ref, cout_ref.at[pl.ds(k * height, height)])
        cs_new[k * tiles : (k + 1) * tiles, :] = state_ref[...]
    base = (n - 1) * tiles
    result = update_context(base, *unpack_message(msgs[-1]), v_ref, w_ref, q_ref, last_pt)
    for c, (new_rows, new_state) in enumerate(result):
        c_new[c * TILE : (c + 1) * TILE, :] = new_rows
        cs_new[base + c : base + c + 1, :] = new_state
    store(c_new, cout_ref.at[pl.ds((n - 1) * height, height)])
    store(cs_new, csout_ref)
    c_bf = jnp.concatenate([msg[:height, :] for msg in msgs], axis=0)
    pt_refs = [done[3 * k] for k in range(n - 1)] + [last_pt]
    eye = eye_mask()
    for r in range(rt):
        rows = slice(r * TILE, (r + 1) * TILE)
        pt = jnp.concatenate([ref[:, rows] for ref in pt_refs], axis=0)
        new_rows, new_state = adagrad(eye, v32_ref[rows, :], vs_ref[r : r + 1, :], dot(pt, c_bf, TN))
        v_new[rows, :] = new_rows
        vs_new[r : r + 1, :] = new_state
        store(v_new.at[pl.ds(r * TILE, TILE)], vout_ref.at[pl.ds(r * TILE, TILE)])
    store(vs_new, vsout_ref)
    for copy in stores:
        copy.wait()


def fill_counts(stop, neg_ref, out_ref, q_ref):
    per_stop, rt = neg_ref.shape[1:]
    for pair in range(PAIRS):
        count = jnp.int32(0)
        for n in range(per_stop):
            count += (neg_ref[stop, n, pair % rt] == pair // rt).astype(jnp.int32)
        value = 0.25 * count.astype(F32)
        q_ref[pair : pair + 1, :] = jnp.full((1, TILE), value)
        out_ref[pair] = jnp.full((TILE, TILE), value)


def add_tiles(out_ref, tiles):
    for pair, tile in tiles:
        out_ref[pair] += 0.5 * tile.astype(F32).T


def near_kernel(own_ref, one_ref, neg_ref, near_ref, out_ref, q_ref):
    fill_counts(0, neg_ref, out_ref, q_ref)
    cap = near_ref.shape[0] // 2
    add_tiles(
        out_ref,
        [(ref[slot, 0], near_ref[k * cap + slot]) for k, ref in enumerate((own_ref, one_ref)) for slot in range(cap)],
    )


def first_weights_kernel(own_ref, one_ref, part_ref, two_ref, three_ref, out_ref, ids_ref, scalars, turned, sem):
    msgs = two_ref, three_ref
    cap = (two_ref.shape[0] - TAIL) // TILE
    for at, msg in enumerate(msgs):
        ids_ref[at + 2] = msg[cap * TILE :, :].astype(F32)[:ID_ROWS].astype(jnp.int32)
    copy = pltpu.make_async_copy(ids_ref.at[pl.ds(2, 2)], scalars, sem)
    copy.start()
    ids_ref[0] = own_ref[...]
    ids_ref[1] = one_ref[...]
    places = [(at, slot) for at in range(2) for slot in range(cap)]
    for k, (at, slot) in enumerate(places):
        turned[k] = 0.5 * msgs[at][slot * TILE : (slot + 1) * TILE, :].astype(F32).T
    copy.wait()
    for k, (at, slot) in enumerate(places):
        out_ref[scalars[at, slot, 0]] += turned[k]


def weights_kernel(stop, ids_ref, neg_ref, near_ref, far_ref, out_ref, q_ref):
    fill_counts(stop, neg_ref, out_ref, q_ref)
    cap = far_ref.shape[0] // 2
    tiles = [ref[t] for ref in (near_ref, far_ref) for t in range(2 * cap)]
    add_tiles(out_ref, [(ids_ref[at // cap, at % cap, stop], tile) for at, tile in enumerate(tiles)])


def pack_kernel(me_ref, w_ref, rows_ref, cols_ref, counts_ref, *refs):
    groups, _, cap = w_ref.shape[:3]
    outs, (given, counts, ids, sem) = refs[:4], refs[4:]
    msgs = outs[2:]
    me = me_ref[0]
    fetches = [
        pltpu.make_async_copy(rows_ref, given.at[0], sem.at[0]),
        pltpu.make_async_copy(cols_ref, given.at[1], sem.at[1]),
        pltpu.make_async_copy(counts_ref, counts, sem.at[2]),
    ]
    for copy in fetches:
        copy.start()
    copies = [
        pltpu.make_async_copy(
            w_ref.at[me ^ (at + 2), 0, slot], msg.at[pl.ds(slot * TILE, TILE)], sem.at[3 + at * cap + slot]
        )
        for at, msg in enumerate(msgs)
        for slot in range(cap)
    ]
    for copy in copies:
        copy.start()
    ids[...] = jnp.zeros_like(ids)
    for copy in fetches:
        copy.wait()
    stops = counts.shape[1]
    for slot in range(cap):
        code = jnp.where(slot < counts[...], given[1, slot] * ROW_TILES + given[0, slot], PAIRS)
        which = lax.broadcasted_iota(jnp.int32, code.shape, 0)
        for by in range(groups):
            kept = jnp.sum(jnp.where(which == (me ^ by), code, 0), axis=0, keepdims=True)
            ids[by, slot : slot + 1, :stops] = kept
    outs[0][...] = ids[0, :ID_ROWS]
    outs[1][...] = ids[1, :ID_ROWS]
    for at, msg in enumerate(msgs):
        msg[cap * TILE :, :] = ids[at + 2].astype(F32).astype(BF16)
    for copy in copies:
        copy.wait()


def relay_kernel(wanted, me_ref, w_ref, sib_ref, after_ref, *refs):
    *out_refs, sem = refs
    me = me_ref[0]
    cap = w_ref.shape[2]
    copies = []
    for n, (dst, (by, stop)) in enumerate(zip(out_refs, wanted)):
        for half, src in enumerate((w_ref, sib_ref)):
            copies.append(
                pltpu.make_async_copy(
                    src.at[me ^ by, stop], dst.at[pl.ds(half * cap, cap)], sem.at[2 * n + half]
                )
            )
    for copy in copies:
        copy.start()
    for copy in copies:
        copy.wait()


def params(room=ROOM):
    return pltpu.CompilerParams(vmem_limit_bytes=room)


def context_call(stop, first, last, chunk, v, context, w, q):
    width = v.shape[1]
    height = context[0].shape[0] // CHUNKS if first else context[0].shape[0] - TAIL
    if last:
        outs = [shape(height, width, dtype=F32), shape(height // TILE, TILE, dtype=F32)]
    else:
        outs = [shape(height + TAIL, width)]
    outs = [shape(height, v.shape[0])] + outs
    args = (v, w, q, *context)
    return pl.pallas_call(
        functools.partial(context_kernel, first, last, chunk * height // TILE),
        out_shape=outs,
        in_specs=[VM] * len(args),
        out_specs=[VM] * len(outs),
        compiler_params=params(),
        cost_estimate=FREE,
        name="context_%d_%d" % (stop, chunk),
    )(*args)


def vertex_call(stop, pts, cs, v, vs):
    outs = [shape(*v.shape, dtype=F32), shape(*vs.shape, dtype=F32), shape(*v.shape)]
    return pl.pallas_call(
        functools.partial(vertex_kernel, len(pts), len(cs) == 1),
        out_shape=outs,
        in_specs=[VM] * (len(pts) + len(cs) + 2),
        out_specs=[VM] * len(outs),
        compiler_params=params(),
        cost_estimate=FREE,
        name="vertex_%d" % stop,
    )(*pts, *cs, v, vs)


def final_call(v_bf, w, q, msgs, done, v, vs):
    n = len(msgs)
    height, width = msgs[0].shape[0] - TAIL, v.shape[1]
    tiles = n * height // TILE
    args = (v_bf, w, q, *msgs, *done, v, vs)
    return pl.pallas_call(
        functools.partial(final_kernel, n),
        out_shape=[
            shape(*v.shape, dtype=F32),
            shape(*vs.shape, dtype=F32),
            shape(n * height, width, dtype=F32),
            shape(tiles, TILE, dtype=F32),
        ],
        in_specs=[VM] * len(args),
        out_specs=[HBM] * 4,
        scratch_shapes=[
            pltpu.VMEM((height, v.shape[0]), BF16),
            pltpu.VMEM((height, width), F32),
            pltpu.VMEM((tiles, TILE), F32),
            pltpu.VMEM(v.shape, F32),
            pltpu.VMEM(vs.shape, F32),
            pltpu.SemaphoreType.DMA((n + 2 + v.shape[0] // TILE,)),
        ],
        compiler_params=params(),
        cost_estimate=FREE,
        name="final",
    )(*args)


def weights_call(stop, ids, neg, near, far):
    return pl.pallas_call(
        functools.partial(weights_kernel, stop),
        out_shape=[shape(PAIRS + 1, TILE, TILE, dtype=F32), shape(PAIRS, TILE, dtype=F32)],
        in_specs=[SM] * 2 + [VM] * 2,
        out_specs=[VM] * 2,
        compiler_params=params(),
        cost_estimate=FREE,
        name="weights_%d" % stop,
    )(ids, neg, near, far)


def relay_call(wanted, me, weights, sibling, after):
    cap = weights.shape[2]
    return pl.pallas_call(
        functools.partial(relay_kernel, wanted),
        out_shape=[shape(2 * cap, TILE, TILE)] * len(wanted),
        in_specs=[SM, HBM, HBM, HBM],
        out_specs=[VM] * len(wanted),
        scratch_shapes=[pltpu.SemaphoreType.DMA((2 * len(wanted),))],
        compiler_params=params(),
        cost_estimate=FREE,
        name="relay_%d" % wanted[0][1],
    )(me, weights, sibling, after)


def shifted(value, axis, by):
    peers = lax.axis_size(axis)
    return lax.ppermute(value, axis, [(i, (i + by) % peers) for i in range(peers)])


def swapped(value, by):
    peers = lax.axis_size("group")
    return lax.ppermute(value, "group", [(i, i ^ by) for i in range(peers)])


def shape(*dims, dtype=BF16):
    return jax.ShapeDtypeStruct(dims, dtype)


def body(vertex, vertex_state, context, context_state, tile_weights, tile_rows, tile_cols, tile_counts, negatives):
    weights = tile_weights[0, 0]
    groups, stops, cap = weights.shape[:3]
    rt, ct = vertex.shape[0] // TILE, context.shape[0] // TILE
    assert (groups, rt, rt * ct) == (4, ROW_TILES, PAIRS)
    me = lax.axis_index("group").astype(jnp.int32).reshape(1)
    neg = jnp.transpose(negatives[0, 0], (0, 2, 1))

    outs = [shape(ID_ROWS, TILE, dtype=jnp.int32)] * 2 + [shape(cap * TILE + TAIL, TILE)] * 2
    own_ids, one_ids, *msgs = pl.pallas_call(
        pack_kernel,
        out_shape=outs,
        in_specs=[SM, HBM, HBM, HBM, HBM],
        out_specs=[VM] * len(outs),
        scratch_shapes=[
            pltpu.VMEM((2, cap, groups, stops), jnp.int32),
            pltpu.VMEM((groups, stops), jnp.int32),
            pltpu.VMEM((groups, TAIL, TILE), jnp.int32),
            pltpu.SemaphoreType.DMA((3 + 2 * cap,)),
        ],
        compiler_params=params(PACK_ROOM),
        cost_estimate=FREE,
        name="pack",
    )(
        me,
        weights,
        jnp.transpose(tile_rows[0, 0], (2, 0, 1)),
        jnp.transpose(tile_cols[0, 0], (2, 0, 1)),
        tile_counts[0, 0],
    )
    later, _ = lax.optimization_barrier((weights, msgs[0]))
    sibling = swapped(later, 1)
    two, three, one_ids = swapped(msgs[0], 2), swapped(msgs[1], 3), swapped(one_ids, 1)

    far, near, near_first = relay_call(((2, 1), (0, 1), (0, 0)), me, weights, sibling, one_ids)
    arrived = {1: (near, swapped(far, 2))}
    part, q = pl.pallas_call(
        near_kernel,
        out_shape=[shape(PAIRS + 1, TILE, TILE, dtype=F32), shape(PAIRS, TILE, dtype=F32)],
        in_specs=[SM, SM, SM, VM],
        out_specs=[VM] * 2,
        compiler_params=params(),
        cost_estimate=FREE,
        name="near_0",
    )(own_ids, one_ids, neg, near_first)
    w_sum, ids = pl.pallas_call(
        first_weights_kernel,
        out_shape=[shape(PAIRS + 1, TILE, TILE, dtype=F32), shape(groups, ID_ROWS, TILE, dtype=jnp.int32)],
        in_specs=[VM] * 5,
        out_specs=[VM] * 2,
        scratch_shapes=[
            pltpu.SMEM((2, ID_ROWS, TILE), jnp.int32),
            pltpu.VMEM((2 * cap, TILE, TILE), F32),
            pltpu.SemaphoreType.DMA,
        ],
        input_output_aliases={2: 0},
        compiler_params=params(),
        cost_estimate=FREE,
        name="weights_0",
    )(own_ids, one_ids, part, two, three)

    v, vs = vertex, vertex_state.reshape(rt, TILE)
    v_bf = vertex
    full = (context, context_state.reshape(ct, TILE))
    held = None
    for stop in range(stops - 1):
        pts, sent = [], []
        for chunk in range(CHUNKS):
            given = full if stop == 0 else (held[chunk],)
            pt, new = context_call(stop, stop == 0, False, chunk, v_bf, given, w_sum, q)
            pts.append(pt)
            sent.append(shifted(new, "blk", 1))
        w_sum, q = weights_call(stop + 1, ids, neg, *arrived[stop + 1])
        v, vs, v_bf = vertex_call(stop, pts, [context] if stop == 0 else held, v, vs)
        if stop + 2 < stops:
            if stop == 0:
                wanted = tuple((by, later) for later in range(2, stops) for by in (2, 0))
                pieces = relay_call(wanted, me, weights, sibling, vs)
            far, _ = lax.optimization_barrier((pieces[2 * stop], vs))
            arrived[stop + 2] = (pieces[2 * stop + 1], swapped(far, 2))
        held = sent
    done = []
    for chunk in range(CHUNKS - 1):
        done += context_call(stops - 1, False, True, chunk, v_bf, (held[chunk],), w_sum, q)
    v, vs, c_out, cs_out = final_call(v_bf, w_sum, q, held, done, v, vs)
    return v, vs.reshape(-1), c_out, cs_out.reshape(-1)


def solution(mesh):
    in_specs = (
        P(("group", "blk"), None),
        P(("group", "blk")),
        P(("group", "blk"), None),
        P(("group", "blk")),
        P("group", "blk", None, None, None, None, None),
        P("group", "blk", None, None, None),
        P("group", "blk", None, None, None),
        P("group", "blk", None, None),
        P("group", "blk", None, None, None),
    )
    out_specs = (
        P(("group", "blk"), None),
        P(("group", "blk")),
        P(("group", "blk"), None),
        P(("group", "blk")),
    )
    return jax.shard_map(body, mesh=mesh, in_specs=in_specs, out_specs=out_specs, check_vma=False)
```
